128 devices in a mesh: dp: 4 (over z_lo, core), expert: 32 (over z_hi, x, y).
Axes of the slice: x: 4, y: 4, z: 4 (z_hi: 2, z_lo: 2; z = z_hi * 2 + z_lo), core: 2. Of those that a mesh axis runs over, the one named last changes fastest.
Arguments:
- tokens: bfloat16 [16384, 2048], P(('dp', 'expert')), may hold values from -6 to 6
- out_grad: bfloat16 [16384, 2048], P(('dp', 'expert')), may hold values from -6 to 6
- routes: int32 [16384, 8], P(('dp', 'expert')), may hold values from 0 to 31, all different within a row; in each aligned block of 128 rows (0 to 127, 128 to 255, ...) at most 64 rows name the same one
- probs: bfloat16 [16384, 8], P(('dp', 'expert')), may hold values from 0.019897461 to 1
- w_gate_up: bfloat16 [32, 2048, 768], P('expert'), may hold values from -0.125 to 0.125
- w_down: bfloat16 [32, 384, 2048], P('expert'), may hold values from -0.3125 to 0.3125
- moment_one: float32 [4, 32, 384, 2048], P('dp', 'expert'), may hold values from -12 to 12
- moment_two: float32 [4, 32, 384, 2048], P('dp', 'expert'), may hold values from 1 to 64
- replicas: int32 [32, 4], P('expert'), may hold values from 0 to 1, as said below
- leader: int32 [32], P('expert'), may hold values from 0 to 3
Outputs:
- token_grad: bfloat16 [16384, 2048], P(('dp', 'expert'))
- prob_grad: bfloat16 [16384, 8], P(('dp', 'expert'))
- new_down: bfloat16 [4, 32, 384, 2048], P('dp', 'expert')
- new_moment_one: float32 [4, 32, 384, 2048], P('dp', 'expert')
- new_moment_two: float32 [4, 32, 384, 2048], P('dp', 'expert')
The draws below stay inside these ranges and needn't reach their ends.
Inputs may be any that keep to these rules, and one draw needn't show every extreme that they name: `routes`: in the 128 rows of one device no expert is named by more than 64 rows. Each expert has one to 4 live replicas, its lead among them.
All inputs are finite; a program needn't handle non-finite values.
Results may differ from the reference program's by a relative error of at most 0.0064.
Values may be sent and summed in bfloat16 or wider, within the bound.
A program may use at most 128 MiB of HBM per device.

```python
import math
import jax
import jax.numpy as jnp
import numpy as np
from jax import lax

D = 2048
FF_WIN = 384
TOP = 8
TOK_DEV = 128
EXPERTS = 32
TOKENS = 16384
CAP = 64
N_DP = 4
N_EXPERT = 32


def replica_sets(key):
    base = jax.random.fold_in(key, 7311)
    lead_key, keep_key = jax.random.split(base)
    leader = jax.random.randint(lead_key, (EXPERTS,), 0, N_DP).astype(jnp.int32)
    keeping = jax.random.randint(keep_key, (EXPERTS, N_DP), 0, 2).astype(jnp.int32)
    lead_hot = (jnp.arange(N_DP, dtype=jnp.int32)[None, :] == leader[:, None]).astype(jnp.int32)
    return (leader, jnp.maximum(keeping, lead_hot))


def draw_replicas(key, part):
    return replica_sets(key)[1]


def draw_leader(key, part):
    return replica_sets(key)[0]


def block_levels(stream_key, shape, pieces, smallest, top_value):
    def one(axis_at, blocks):
        draws = jax.random.uniform(jax.random.fold_in(jax.random.fold_in(stream_key, 6), axis_at), (blocks,), jnp.float32, smallest / len(pieces), top_value / len(pieces))
        return jnp.repeat(jnp.exp(draws), shape[axis_at] // blocks).reshape((-1,) + (1,) * (len(shape) - axis_at - 1))

    gain = one(*pieces[0])
    for cut in pieces[1:]:
        gain = gain * one(*cut)
    return gain


def deal_out(stream_key, own, number, rows, number_of, top, limit, lean):
    ranking = jax.random.permutation(stream_key, number_of)
    crowded, common = load_shares(number_of, rows * top, limit, lean, True), load_shares(number_of, rows * top, limit, lean, False)
    places = jnp.arange(number_of)

    def named(lengths, turn):
        used = int((lengths > 0).sum())
        fixed = max(1, used // 4)
        shifted = fixed + (places - fixed + turn * (used - fixed)) % max(1, number_of - fixed)
        return jnp.zeros((number_of,), jnp.int32).at[ranking[jnp.where(places < fixed, places, shifted)]].set(jnp.asarray(lengths, jnp.int32))

    lengths = jnp.where(number % 4 == 0, named(crowded, number // 4), named(common, number - number // 4 - 1))
    mixed = jax.random.permutation(jax.random.fold_in(own, 3), number_of)
    donor, sink = mixed[0:number_of // 2 * 2:2], mixed[1:number_of // 2 * 2:2]
    margin = jnp.minimum(lengths[donor] - 1, limit - lengths[sink]) // 2
    margin = jnp.where((donor == ranking[0]) | (sink == ranking[0]) | (lengths[sink] == 0), 0, jnp.maximum(margin, 0))
    shifted = jax.random.randint(jax.random.fold_in(own, 4), (number_of // 2,), 0, 1 << 20) % (margin + 1)
    lengths = lengths.at[donor].add(-shifted).at[sink].add(shifted)
    items = jnp.searchsorted(jnp.cumsum(lengths), jnp.arange(rows * top), side="right").astype(jnp.int32)
    grid = items.reshape(top, rows).T
    grid = grid[jax.random.permutation(jax.random.fold_in(own, 1), rows)]
    turn = jax.random.randint(jax.random.fold_in(own, 2), (rows, 1), 0, top)
    return jnp.take_along_axis(grid, (jnp.arange(top)[None, :] + turn) % top, axis=1)


def load_shares(amount, total, reach, lean, full):
    loads = [(1 << 20) // math.isqrt(grade ** lean) + 1 for grade in range(1, amount + 1)]
    largest = reach if full else min(reach, max(-(-total // amount), total * loads[0] // sum(loads)))
    least = 1 if total - largest >= amount - 1 else 0
    holding, rest = [largest] + [least] * (amount - 1), total - largest - least * (amount - 1)
    while rest > 0:
        movable = [i for i in range(1, amount) if holding[i] < largest] or [i for i in range(1, amount) if holding[i] < reach]
        whole, left = sum([loads[i] for i in movable]), rest
        for i in movable:
            extra = min(reach - holding[i], max(1, left * loads[i] // whole), rest)
            holding[i] = holding[i] + extra
            rest = rest - extra
    return np.array(holding)


def centred(own_key, shape, deviation, bound, shards=(), kind=jnp.bfloat16):
    drawn = jax.random.normal(own_key, shape, jnp.float32) * deviation
    if len(shards) > 0:
        drawn = block_levels(own_key, shape, shards, -0.22, 0.18) * drawn
    return jnp.clip(drawn, min=-bound, max=bound).astype(kind)


def setup_inputs(seed: int = 0) -> dict:
    key_of = jax.random.split(jax.random.key(seed), 11)
    tokens = centred(key_of[0], (TOKENS, D), 1.0, 6.0, ((0, 128),))
    out_grad = centred(key_of[1], (TOKENS, D), 1.0, 6.0, ((0, 128),))
    routes_keys = jax.random.split(jax.random.fold_in(key_of[2], 1), TOKENS // TOK_DEV)
    routes_turns = jax.random.permutation(jax.random.fold_in(key_of[2], 3), TOKENS // TOK_DEV)
    routes = jax.vmap(lambda own, number: deal_out(jax.random.fold_in(key_of[2], 2), own, number, TOK_DEV, EXPERTS, TOP, CAP, 2))(routes_keys, routes_turns).reshape((TOKENS, TOP))
    probs = jnp.clip(jnp.exp(math.log(1.0) - 3.9171631 * jax.random.uniform(key_of[3], (TOKENS, TOP), jnp.float32) ** block_levels(key_of[3], (TOKENS, TOP), ((0, 128),), -0.2, 0.2)), 0.019897461, 1.0).astype(jnp.bfloat16)
    w_gate_up = centred(key_of[4], (EXPERTS, D, 2 * FF_WIN), D ** -0.5, 0.125, ((0, 32),))
    w_down = centred(key_of[5], (EXPERTS, FF_WIN, D), FF_WIN ** -0.5, 0.3125, ((0, 32),))
    moment_one = centred(key_of[6], (N_DP, EXPERTS, FF_WIN, D), 2.0, 12.0, ((0, 4), (1, 32)), jnp.float32)
    moment_two = jnp.clip(jnp.exp(math.log(64.0) - 4.158883 * jax.random.uniform(key_of[7], (N_DP, EXPERTS, FF_WIN, D), jnp.float32) ** block_levels(key_of[7], (N_DP, EXPERTS, FF_WIN, D), ((0, 4), (1, 32)), -0.2, 0.2)), 1.0, 64.0)
    replicas = draw_replicas(jax.random.fold_in(key_of[10], 71), 0)
    leader = draw_leader(jax.random.fold_in(key_of[10], 71), 0)
    return dict(tokens=tokens, out_grad=out_grad, routes=routes, probs=probs, w_gate_up=w_gate_up, w_down=w_down, moment_one=moment_one, moment_two=moment_two, replicas=replicas, leader=leader)


learn_rate = 0.01
beta_one = 0.9
beta_two = 0.95
adam_eps = 1e-08
weight_decay = 0.1
adam_step = 100

def expert_rows(gate_up, grads, weights, w_gu, w_dn):
    half = w_dn.shape[0]
    gate = gate_up[:, :half]
    upper = gate_up[:, half:]
    sigma = jax.nn.sigmoid(gate)
    silu_val = gate * sigma
    hidden = (silu_val * upper).astype(jnp.bfloat16)
    grads_wide = grads.astype(jnp.float32)
    scaled = (weights.astype(jnp.float32)[:, None] * grads_wide).astype(jnp.bfloat16)
    output = jnp.dot(hidden, w_dn, preferred_element_type=jnp.float32)
    pair_prob = lax.optimization_barrier(jnp.sum(grads_wide * output, axis=1)).astype(jnp.bfloat16)
    hidden_grad = lax.dot_general(scaled, w_dn, (((1,), (1,)), ((), ())), preferred_element_type=jnp.float32)
    deriv = sigma * (1.0 + gate * (1.0 - sigma))
    pre_grad = jnp.concatenate([hidden_grad * upper * deriv, hidden_grad * silu_val], axis=1).astype(jnp.bfloat16)
    pair_grad = lax.dot_general(pre_grad, w_gu, (((1,), (1,)), ((), ())), preferred_element_type=jnp.float32).astype(jnp.bfloat16)
    weight_grad = lax.dot_general(hidden, scaled, (((0,), (0,)), ((), ())), preferred_element_type=jnp.float32)
    return (pair_grad, pair_prob, weight_grad)

def adam_update(grad, m_old, v_old, w_old):
    m_new = beta_one * m_old + (1.0 - beta_one) * grad
    v_new = beta_two * v_old + (1.0 - beta_two) * grad * grad
    m_hat = m_new / (1.0 - beta_one ** adam_step)
    v_hat = v_new / (1.0 - beta_two ** adam_step)
    w_wide = w_old.astype(jnp.float32)
    w_new = (w_wide - learn_rate * (m_hat / (jnp.sqrt(v_hat) + adam_eps) + weight_decay * w_wide)).astype(jnp.bfloat16)
    return (m_new, v_new, w_new)

def reference(tokens, out_grad, routes, probs, w_gate_up, w_down, moment_one, moment_two, replicas, leader):
    assign_count = TOKENS * TOP
    most_rows = N_DP * N_EXPERT * CAP
    flat = routes.reshape(-1).astype(jnp.int32)
    flat_probs = probs.reshape(-1)
    padded_tokens = jnp.concatenate([tokens, jnp.zeros((1, D), jnp.bfloat16)], axis=0)
    padded_grads = jnp.concatenate([out_grad, jnp.zeros((1, D), jnp.bfloat16)], axis=0)

    def per_expert(carry, expert_id):
        token_acc, prob_acc = carry
        picks = jnp.nonzero(flat == expert_id, size=most_rows, fill_value=assign_count)[0].astype(jnp.int32)
        valid = picks < assign_count
        token_of = jnp.where(valid, picks // TOP, TOKENS).astype(jnp.int32)
        inputs = padded_tokens[token_of]
        grads = padded_grads[token_of]
        safe = jnp.minimum(picks, assign_count - 1).astype(jnp.int32)
        weights = jnp.where(valid, flat_probs[safe], jnp.zeros((), jnp.bfloat16))
        gate_up = jnp.dot(inputs, w_gate_up[expert_id], preferred_element_type=jnp.float32)
        pair_grad, pair_prob, weight_grad = expert_rows(gate_up, grads, weights, w_gate_up[expert_id], w_down[expert_id])
        token_acc = token_acc.at[token_of].add(pair_grad.astype(jnp.float32), mode='drop')
        prob_acc = prob_acc.at[picks].set(pair_prob, mode='drop')
        return ((token_acc, prob_acc), weight_grad)
    start = (jnp.zeros((TOKENS, D), jnp.float32), jnp.zeros((assign_count,), jnp.bfloat16))
    (token_acc, prob_acc), grad_down = lax.scan(per_expert, start, jnp.arange(EXPERTS, dtype=jnp.int32))
    token_grad = token_acc.astype(jnp.bfloat16)
    prob_grad = prob_acc.reshape(TOKENS, TOP)
    expert_ids = jnp.arange(EXPERTS, dtype=jnp.int32)
    lead_m = moment_one[leader, expert_ids]
    lead_v = moment_two[leader, expert_ids]
    m_new, v_new, w_new = adam_update(grad_down, lead_m, lead_v, w_down)
    is_lead = (jnp.arange(N_DP, dtype=jnp.int32)[:, None] == leader[None, :])[:, :, None, None]
    live = (jnp.transpose(replicas) == 1)[:, :, None, None]
    new_down = jnp.where(live, w_new[None], w_down[None])
    new_moment_one = jnp.where(is_lead, m_new[None], moment_one)
    new_moment_two = jnp.where(is_lead, v_new[None], moment_two)
    return (token_grad, prob_grad, new_down, new_moment_one, new_moment_two)
```

```python
import jax
import jax.numpy as jnp
from jax import lax
from jax.experimental import pallas as pl
from jax.experimental.pallas import tpu as pltpu
from jax.sharding import PartitionSpec as P

F32, BF = jnp.float32, jnp.bfloat16
MESH = pl.DeviceIdType.MESH
learn_rate = 0.01
beta_one = 0.9
beta_two = 0.95
adam_eps = 1e-08
weight_decay = 0.1
adam_step = 100


def place():
    dp = lax.axis_index("dp")
    ex = lax.axis_index("expert")
    return dp // 2, dp % 2, ex // 16, (ex // 4) % 4, ex % 4


def greet(peers):
    barrier = pltpu.get_barrier_semaphore()
    for peer in peers:
        pl.semaphore_signal(barrier, inc=1, device_id=peer, device_id_type=MESH)
    pl.semaphore_wait(barrier, len(peers))


def gather_kernel(tok, grad, pst, wgu, wdn, mv, gx, gd, prec, fgu, fdn, mvs, own, ownp, own_sem, psend, precv, asend, arecv, wsend, wrecv):
    zl, co, h, x, y = place()
    me = x * 4 + y
    dp = zl * 2 + co
    dev = lambda d, hh, i: (d, hh * 16 + i)
    sibling = (zl * 2 + 1 - co, h * 16 + me)
    cross = ((1 - zl) * 2 + co, (1 - h) * 16 + me)
    zside = ((1 - zl) * 2 + co, h * 16 + me)
    plane = [dev(dp, h, (me + r) % 16) for r in range(1, 16)]
    inputs = (tok, grad)
    keep_in = [pltpu.make_async_copy(inputs[a], own.at[a], own_sem.at[a]) for a in range(2)]
    for c in keep_in:
        c.start()
    own_p = pltpu.make_async_copy(pst.at[me], ownp, psend.at[0])
    own_p.start()
    greet(plane + [sibling, cross, zside])

    def rdma(src, dst, s, r, peer):
        c = pltpu.make_async_remote_copy(src, dst, s, r, device_id=peer, device_id_type=MESH)
        c.start()
        return c

    pending = []
    rows_gu = pl.ds(co * 1024, 1024)
    rows_dn = pl.ds(co * 192, 192)
    w1 = rdma(wgu.at[0, rows_gu], fgu.at[rows_gu], wsend.at[0], wrecv.at[0], cross)
    w2 = rdma(wdn.at[0, rows_dn], fdn.at[rows_dn], wsend.at[1], wrecv.at[1], cross)
    m1 = rdma(mv, mvs.at[dp], wsend.at[2], wrecv.at[2], zside)
    m2 = rdma(mv, mvs.at[dp], wsend.at[3], wrecv.at[3], sibling)
    for r in range(1, 16):
        pending.append(rdma(pst.at[(me + r) % 16], prec.at[me], psend.at[r], precv.at[r], plane[r - 1]))

    outs = (gx, gd)

    def spot(a, i, j):
        return (i % 4) * 4 + j % 4 if a == 0 else (j % 4) * 4 + i % 4

    def peer_at(a, i, j):
        return dev(dp, h, spot(a, i, j))

    pos = ((x, y), (y, x))
    lo, hi = pl.ds(0, 64), pl.ds(64, 64)
    copies = [[None] * 20, [None] * 20]

    def send(a, k, src, dst, peer):
        copies[a][k] = rdma(src, dst, asend.at[a, k], arecv.at[a, k], peer)

    def send_full(a, k, block, src, i, j, first):
        left = peer_at(a, i - 1, j) if first else peer_at(a, i, j - 1)
        right = peer_at(a, i + 1, j) if first else peer_at(a, i, j + 1)
        send(a, k, src, outs[a].at[block], right)
        send(a, k + 1, src, outs[a].at[block], left)

    def pass_on(a, k, block, i, j, first):
        o = outs[a]
        copies[a][k].wait_recv()
        lblock, rblock = block
        right = peer_at(a, i + 1, j) if first else peer_at(a, i, j + 1)
        left = peer_at(a, i - 1, j) if first else peer_at(a, i, j - 1)
        send(a, k + 2, o.at[lblock, lo], o.at[lblock, lo], right)
        copies[a][k + 1].wait_recv()
        send(a, k + 3, o.at[rblock, hi], o.at[rblock, hi], left)

    for a in range(2):
        i, j = pos[a]
        send_full(a, 0, me, inputs[a], i, j, True)
    for a in range(2):
        i, j = pos[a]
        send_full(a, 4, me, inputs[a], i, j, False)
    keep_out = []
    for a in range(2):
        keep_in[a].wait()
        c = pltpu.make_async_copy(own.at[a], outs[a].at[me], own_sem.at[a])
        c.start()
        keep_out.append(c)
    own_p.wait()
    own_p = pltpu.make_async_copy(ownp, prec.at[me], precv.at[0])
    own_p.start()
    keep_out.append(own_p)
    for a in range(2):
        i, j = pos[a]
        pass_on(a, 0, (spot(a, i - 1, j), spot(a, i + 1, j)), i, j, True)
    for a in range(2):
        i, j = pos[a]
        for n, s in ((1, -1), (2, 1)):
            b = spot(a, i + s, j)
            send_full(a, 4 + 4 * n, b, outs[a].at[b], i, j, False)
    for a in range(2):
        i, j = pos[a]
        pass_on(a, 4, (spot(a, i, j - 1), spot(a, i, j + 1)), i, j, False)
    for a in range(2):
        i, j = pos[a]
        copies[a][2].wait_recv()
        copies[a][3].wait_recv()
        b = spot(a, i + 2, j)
        send_full(a, 16, b, outs[a].at[b], i, j, False)
    for n, s in ((1, -1), (2, 1), (3, 2)):
        for a in range(2):
            i, j = pos[a]
            pass_on(a, 4 + 4 * n, (spot(a, i + s, j - 1), spot(a, i + s, j + 1)), i, j, False)
        if n == 2:
            w1.wait_recv()
            v1 = rdma(fgu.at[rows_gu], fgu.at[rows_gu], wsend.at[4], wrecv.at[4], sibling)
            w2.wait_recv()
            v2 = rdma(fdn.at[rows_dn], fdn.at[rows_dn], wsend.at[5], wrecv.at[5], sibling)
    m1.wait_recv()
    zdp = (1 - zl) * 2 + co
    m3 = rdma(mvs.at[zdp], mvs.at[zdp], wsend.at[6], wrecv.at[6], sibling)
    for a in range(2):
        for k in range(4, 20, 4):
            copies[a][k + 2].wait_recv()
            copies[a][k + 3].wait_recv()
    for c in (m2, m3, v1, v2):
        c.wait_recv()
    for c in pending:
        c.wait_recv()
    for c in keep_out:
        c.wait()
    for a in range(2):
        for c in copies[a]:
            c.wait_send()
    for c in [w1, w2, m1, m2, m3, v1, v2] + pending:
        c.wait_send()


def gather(tok, grad, pst, wgu, wdn, mv):
    bf = jnp.bfloat16
    any_ = pl.BlockSpec(memory_space=pl.ANY)
    sd = jax.ShapeDtypeStruct
    return pl.pallas_call(
        gather_kernel,
        name="gather_rows",
        out_shape=(sd((16, 128, 2048), bf), sd((16, 128, 2048), bf), sd((16, 8, 128), jnp.float32),
                   sd((2048, 768), bf), sd((384, 2048), bf), sd((4, 2, 384, 2048), bf)),
        in_specs=[any_] * 6,
        out_specs=(any_,) * 6,
        scratch_shapes=[
            pltpu.VMEM((2, 128, 2048), bf),
            pltpu.VMEM((8, 128), jnp.float32),
            pltpu.SemaphoreType.DMA((2,)),
            pltpu.SemaphoreType.DMA((16,)),
            pltpu.SemaphoreType.DMA((16,)),
            pltpu.SemaphoreType.DMA((2, 20)),
            pltpu.SemaphoreType.DMA((2, 20)),
            pltpu.SemaphoreType.DMA((7,)),
            pltpu.SemaphoreType.DMA((7,)),
        ],
        compiler_params=pltpu.CompilerParams(collective_id=0, has_side_effects=True),
    )(tok, grad, pst, wgu, wdn, mv)


def nt(a, b):
    return lax.dot_general(a, b, (((1,), (1,)), ((), ())), preferred_element_type=F32)


def tn(a, b):
    return lax.dot_general(a, b, (((0,), (0,)), ((), ())), preferred_element_type=F32)


def expert_kernel(gx, gd, prec, wgu, wdn, fgu, fdn, dout, gout, qout,
                  xs, ds, gus, dns, xc, dc, oall, opall, ps, gu_s, g_s, pre_s, hid_s, stage, in_sem, w_sem, out_sem):
    def feed(c):
        rows = pl.ds(c * 8, 8)
        return (pltpu.make_async_copy(gx.at[rows], xs.at[rows], in_sem.at[0, c]),
                pltpu.make_async_copy(gd.at[rows], ds.at[rows], in_sem.at[1, c]))

    weights = (pltpu.make_async_copy(wgu.at[0], gus.at[0], w_sem.at[0]),
               pltpu.make_async_copy(wdn.at[0], dns.at[0], w_sem.at[1]),
               pltpu.make_async_copy(fgu, gus.at[1], w_sem.at[2]),
               pltpu.make_async_copy(fdn, dns.at[1], w_sem.at[3]))
    for c in (*feed(0), *weights, *feed(1)):
        c.start()
    oall[...] = jnp.zeros_like(oall)
    opall[...] = jnp.zeros_like(opall)
    gout[...] = jnp.zeros_like(gout)
    qout[...] = jnp.zeros_like(qout)
    before = (lax.broadcasted_iota(jnp.int32, (128, 128), 0) < lax.broadcasted_iota(jnp.int32, (128, 128), 1)).astype(BF)
    slot = lax.broadcasted_iota(jnp.int32, (64, 128), 0).astype(F32)

    def chunk(c, _):
        for f in feed(c):
            f.wait()

        def pack(j, _):
            for i in range(2):
                b = c * 8 + j * 2 + i
                p = prec[b]
                on = (p > 0).astype(F32)
                rank = jnp.dot(on.astype(BF), before, preferred_element_type=F32)
                rank = jnp.where(on > 0, rank, -1.0)
                for e in range(2):
                    hot = rank[e:e + 1, :] == slot
                    oall[j, pl.ds(e * 128 + i * 64, 64), pl.ds(i * 128, 128)] = hot.astype(F32).astype(BF)
                    held = jnp.where(hot, p[e:e + 1, :], 0.0)
                    opall[pl.ds(e * 128 + i * 64, 64), pl.ds(i * 128, 128)] = held.astype(BF)
                    col = jnp.sum(held, axis=1, keepdims=True)
                    ps[e, pl.ds(pl.multiple_of(j * 128 + i * 64, 64), 64), :] = jnp.broadcast_to(col, (64, 128))
            rows = pl.ds(pl.multiple_of(j * 128, 128), 128)
            blocks = pl.ds(c * 8 + j * 2, 2)
            for o, src, dst in ((oall[j], xs, xc), (opall[...], ds, dc)):
                r = jnp.dot(o, src[blocks].reshape(256, 2048), preferred_element_type=F32).astype(BF)
                dst[0, rows] = r[:128]
                dst[1, rows] = r[128:]
            return 0

        lax.fori_loop(0, 4, pack, 0)

        @pl.when(c == 0)
        def _():
            for w in weights:
                w.wait()

        def expert(e, _):
            gu_s[...] = jnp.dot(xc[e], gus[e], preferred_element_type=F32)
            g_s[...] = nt(dc[e], dns[e])

            def mid(t, _):
                rows = pl.ds(pl.multiple_of(t * 64, 64), 64)
                gate, up, g = gu_s[rows, :384], gu_s[rows, 384:], g_s[rows]
                p = ps[e, rows, :1]
                sig = jax.nn.sigmoid(gate)
                silu = gate * sig
                hid = silu * up
                hid = hid.astype(BF)
                q = jnp.sum(hid.astype(F32) * g, axis=1, keepdims=True) / jnp.where(p > 0, p, 1.0)
                hid_s[rows] = hid
                pre_s[rows, :384] = (g * up * (sig * (1.0 + gate * (1.0 - sig)))).astype(BF)
                pre_s[rows, 384:] = (g * silu).astype(BF)
                ps[e, rows, :] = jnp.broadcast_to(q, (64, 128))
                return 0

            lax.fori_loop(0, 8, mid, 0)
            gout[e] += tn(hid_s[...], dc[e])
            xc[e] = nt(pre_s[...], gus[e]).astype(BF)
            return 0

        lax.fori_loop(0, 2, expert, 0)

        def spread(j, _):
            s = j % 2
            n = c * 4 + j

            def out(k):
                return pltpu.make_async_copy(stage.at[k % 2], dout.at[pl.ds(k * 2, 2)], out_sem.at[k % 2])

            @pl.when(n >= 2)
            def _():
                out(n - 2).wait()

            rows = pl.ds(pl.multiple_of(j * 128, 128), 128)
            o = oall[j]
            y = tn(o[:128], xc[0, rows]) + tn(o[128:], xc[1, rows])
            stage[s] = y.astype(BF).reshape(2, 128, 2048)
            out(n).start()
            for i in range(2):
                for e in range(2):
                    hot = oall[j, pl.ds(e * 128 + i * 64, 64), pl.ds(i * 128, 128)].astype(F32)
                    q = ps[e, pl.ds(pl.multiple_of(j * 128 + i * 64, 64), 64), :]
                    qout[c * 8 + j * 2 + i, e:e + 1, :] = jnp.sum(hot * q, axis=0, keepdims=True)
            return 0

        lax.fori_loop(0, 4, spread, 0)
        return 0

    lax.fori_loop(0, 2, chunk, 0)
    for k in (6, 7):
        pltpu.make_async_copy(stage.at[k % 2], dout.at[pl.ds(k * 2, 2)], out_sem.at[k % 2]).wait()


def experts(gx, gd, prec, wgu, wdn, fgu, fdn):
    any_ = pl.BlockSpec(memory_space=pl.ANY)
    vm = pl.BlockSpec(memory_space=pltpu.VMEM)
    sd = jax.ShapeDtypeStruct
    return pl.pallas_call(
        expert_kernel,
        name="expert_rows",
        out_shape=(sd((16, 128, 2048), BF), sd((2, 384, 2048), F32), sd((16, 8, 128), F32)),
        in_specs=[any_, any_, vm, any_, any_, any_, any_],
        out_specs=(any_, vm, vm),
        scratch_shapes=[
            pltpu.VMEM((16, 128, 2048), BF), pltpu.VMEM((16, 128, 2048), BF),
            pltpu.VMEM((2, 2048, 768), BF), pltpu.VMEM((2, 384, 2048), BF),
            pltpu.VMEM((2, 512, 2048), BF), pltpu.VMEM((2, 512, 2048), BF),
            pltpu.VMEM((4, 256, 256), BF), pltpu.VMEM((256, 256), BF), pltpu.VMEM((2, 512, 128), F32),
            pltpu.VMEM((512, 768), F32), pltpu.VMEM((512, 384), F32),
            pltpu.VMEM((512, 768), BF), pltpu.VMEM((512, 384), BF),
            pltpu.VMEM((2, 2, 128, 2048), BF),
            pltpu.SemaphoreType.DMA((2, 2)), pltpu.SemaphoreType.DMA((4,)), pltpu.SemaphoreType.DMA((2,)),
        ],
        compiler_params=pltpu.CompilerParams(vmem_limit_bytes=64 * 1024 * 1024 - 65536),
    )(gx, gd, prec, wgu, wdn, fgu, fdn)


def return_kernel(d, g, q, tout, gfull, qout, dv, relay, full, part, relay2, full2, gv, near, fsend, frecv, osend, orecv, gsum, qrecv,
                  lsem, s1, r1, s2, r2, ws, wr, qs, qr):
    zl, co, h, x, y = place()
    me = x * 4 + y
    dp = zl * 2 + co
    base = h * 16
    sibling = (zl * 2 + 1 - co, base + me)
    cross = ((1 - zl) * 2 + co, (1 - h) * 16 + me)
    zside = ((1 - zl) * 2 + co, base + me)
    plane = [(dp, base + (me + r) % 16) for r in range(1, 16)]
    pos = ((x, y), (y, x))

    def spot(a, i, j):
        return (i % 4) * 4 + j % 4 if a == 0 else (j % 4) * 4 + i % 4

    def rdma(src, dst, s, r, peer):
        c = pltpu.make_async_remote_copy(src, dst, s, r, device_id=peer, device_id_type=MESH)
        c.start()
        return c

    mine, other = pl.ds(co * 192, 192), pl.ds((1 - co) * 192, 192)
    loads = [pltpu.make_async_copy(d, dv, lsem.at[0])]
    loads += [pltpu.make_async_copy(g.at[e, mine], gv.at[e], lsem.at[1 + e]) for e in range(2)]
    for c in loads:
        c.start()
    greet(plane + [sibling, cross, zside])

    sent = []
    near_in = [[None] * 3 for _ in range(2)]
    for n in range(3):
        for e in (1, 0):
            c = rdma(g.at[e, pl.ds((1 - co) * 192 + n * 64, 64)], near.at[e, pl.ds(n * 64, 64)], ws.at[e, n], wr.at[e, n], sibling)
            near_in[e][n] = c
    order = (2, 1, 3, 0)
    half = (pl.ds(0, 32), pl.ds(32, 32))
    first = {}
    for jj in order:
        for a in range(2):
            i, j = pos[a]
            far = spot(a, i + 2, j + jj)
            for t in range(2):
                peer = (dp, base + spot(a, i + 1 - 2 * t, j))
                first[a, jj, t, 0] = rdma(d.at[far, pl.ds(a * 64 + t * 32, 32)], relay.at[a, jj, t], s1.at[a, jj, t, 0], r1.at[a, jj, t, 0], peer)
    for jj in order:
        for a in range(2):
            i, j = pos[a]
            for t in range(2):
                peer = (dp, base + spot(a, i + 1 - 2 * t, j))
                to = spot(a, i + 1 - 2 * t, j + jj)
                first[a, jj, t, 1] = rdma(d.at[to, pl.ds(a * 64 + (1 - t) * 32, 32)], full.at[a, jj, t, half[1 - t]], s1.at[a, jj, t, 1], r1.at[a, jj, t, 1], peer)
    qc = [rdma(q.at[(me + r) % 16], qrecv.at[me], qs.at[r], qr.at[r], plane[r - 1]) for r in range(1, 16)]
    for c in loads:
        c.wait()

    def add_relay(jj, a, t):
        i, j = pos[a]
        first[a, jj, t, 0].wait_recv()
        to = spot(a, i + 1 - 2 * t, j + jj)
        peer = (dp, base + spot(a, i + 1 - 2 * t, j))
        relay[a, jj, t] = (relay[a, jj, t].astype(F32) + dv[to, a * 64 + t * 32:a * 64 + t * 32 + 32].astype(F32)).astype(BF)
        first[a, jj, t, 2] = rdma(relay.at[a, jj, t], full.at[a, jj, t, half[t]], s1.at[a, jj, t, 2], r1.at[a, jj, t, 2], peer)

    def foreign(n):
        rows = pl.ds(n * 64, 64)
        near_in[1][n].wait_recv()
        fsend[rows] = (gv[1, rows] + near[1, rows]).astype(BF)
        return rdma(fsend.at[rows], frecv.at[rows], ws.at[2, n], wr.at[2, n], cross)

    def ours(n, f):
        rows = pl.ds(n * 64, 64)
        near_in[0][n].wait_recv()
        f.wait_recv()
        v = gv[0, rows] + near[0, rows] + frecv[rows].astype(F32)
        gsum[rows] = v
        osend[rows] = v.astype(BF)
        return rdma(osend.at[rows], orecv.at[rows], ws.at[3, n], wr.at[3, n], zside)

    def whole(n, o):
        rows = pl.ds(n * 64, 64)
        o.wait_recv()
        gsum[rows] = gsum[rows] + orecv[rows].astype(F32)
        out = pl.ds(co * 192 + n * 64, 64)
        loc = pltpu.make_async_copy(gsum.at[rows], gfull.at[out], lsem.at[3 + n])
        loc.start()
        return loc, rdma(gsum.at[rows], gfull.at[out], ws.at[4, n], wr.at[4, n], sibling)

    second = {}

    def line_sum(jj, a):
        i, j = pos[a]
        for t in range(2):
            first[a, jj, t, 1].wait_recv()
            first[a, jj, t, 2].wait_recv()
        at = spot(a, i, j + jj)
        part[a, jj] = (dv[at, a * 64:a * 64 + 64].astype(F32) + full[a, jj, 0].astype(F32) + full[a, jj, 1].astype(F32)).astype(BF)
        side = [(dp, base + spot(a, i, j + 1 - 2 * t)) for t in range(2)]
        if jj == 2:
            for t in range(2):
                second[a, t, 0] = rdma(part.at[a, 2, half[t]], relay2.at[a, t], s2.at[a, t, 0], r2.at[a, t, 0], side[t])
        elif jj != 0:
            t = 0 if jj == 1 else 1
            second[a, t, 1] = rdma(part.at[a, jj, half[1 - t]], full2.at[a, t, half[1 - t]], s2.at[a, t, 1], r2.at[a, t, 1], side[t])
            second[a, t, 0].wait_recv()
            relay2[a, t] = (relay2[a, t].astype(F32) + part[a, jj, t * 32:t * 32 + 32].astype(F32)).astype(BF)
            second[a, t, 2] = rdma(relay2.at[a, t], full2.at[a, t, half[t]], s2.at[a, t, 2], r2.at[a, t, 2], side[t])

    fs, os, gs = [], [], []
    for jj in order:
        for a in range(2):
            for t in range(2):
                add_relay(jj, a, t)
        if jj != 2:
            fs.append(foreign(len(fs)))
    os.append(ours(0, fs[0]))
    for a in range(2):
        line_sum(2, a)
    os.append(ours(1, fs[1]))
    for a in range(2):
        line_sum(1, a)
    os.append(ours(2, fs[2]))
    gs.append(whole(0, os[0]))
    for a in range(2):
        line_sum(3, a)
    gs.append(whole(1, os[1]))
    for a in range(2):
        line_sum(0, a)
    gs.append(whole(2, os[2]))
    for a in range(2):
        for t in range(2):
            second[a, t, 1].wait_recv()
            second[a, t, 2].wait_recv()
        tout[a * 64:a * 64 + 64, :] = (part[a, 0].astype(F32) + full2[a, 0].astype(F32) + full2[a, 1].astype(F32)).astype(BF)
    for c in qc:
        c.wait_recv()
    qrecv[me] = q[me]
    qout[...] = qrecv[...]
    for loc, c in gs:
        loc.wait()
        c.wait_recv()
    for c in list(first.values()) + list(second.values()) + near_in[0] + near_in[1] + fs + os + [c for _, c in gs] + qc:
        c.wait_send()


def give_back(d, g, q):
    any_ = pl.BlockSpec(memory_space=pl.ANY)
    vm = pl.BlockSpec(memory_space=pltpu.VMEM)
    sd = jax.ShapeDtypeStruct
    dma = pltpu.SemaphoreType.DMA
    return pl.pallas_call(
        return_kernel,
        name="return_rows",
        out_shape=(sd((128, 2048), BF), sd((384, 2048), F32), sd((16, 8, 128), F32)),
        in_specs=[any_, any_, vm],
        out_specs=(vm, any_, vm),
        scratch_shapes=[
            pltpu.VMEM((16, 128, 2048), BF),
            pltpu.VMEM((2, 4, 2, 32, 2048), BF), pltpu.VMEM((2, 4, 2, 64, 2048), BF), pltpu.VMEM((2, 4, 64, 2048), BF),
            pltpu.VMEM((2, 2, 32, 2048), BF), pltpu.VMEM((2, 2, 64, 2048), BF),
            pltpu.VMEM((2, 192, 2048), F32), pltpu.VMEM((2, 192, 2048), F32),
            pltpu.VMEM((192, 2048), BF), pltpu.VMEM((192, 2048), BF), pltpu.VMEM((192, 2048), BF), pltpu.VMEM((192, 2048), BF),
            pltpu.VMEM((192, 2048), F32), pltpu.VMEM((16, 8, 128), F32),
            dma((6,)), dma((2, 4, 2, 3)), dma((2, 4, 2, 3)), dma((2, 2, 3)), dma((2, 2, 3)), dma((5, 3)), dma((5, 3)), dma((16,)), dma((16,)),
        ],
        compiler_params=pltpu.CompilerParams(collective_id=1, has_side_effects=True, vmem_limit_bytes=60 * 1024 * 1024),
    )(d, g, q)


def body(tokens, out_grad, routes, probs, w_gate_up, w_down, moment_one, moment_two, replicas, leader):
    rank = lax.axis_index("dp")
    ex = lax.axis_index("expert")
    h = ex // 16
    ids = jnp.arange(32, dtype=jnp.int32)
    hit = routes[None] == ids[:, None, None]
    dense = jnp.sum(jnp.where(hit, probs.astype(F32)[None], 0.0), axis=2).reshape(2, 16, 128)
    near = lax.dynamic_index_in_dim(dense, h, 0, keepdims=False)
    far = lax.dynamic_index_in_dim(dense, 1 - h, 0, keepdims=False)
    pst = jnp.pad(jnp.stack([near, far], axis=1), ((0, 0), (0, 6), (0, 0)))
    m_old, v_old = moment_one[0, 0], moment_two[0, 0]
    mv = jnp.stack([m_old.astype(BF), v_old.astype(BF)])
    gx, gd, prec, fgu, fdn, mvs = gather(tokens, out_grad, pst, w_gate_up, w_down, mv)
    d, g, q = experts(gx, gd, prec, w_gate_up, w_down, fgu, fdn)
    token_grad, grad, qb = give_back(d, g, q)
    whole = qb[:, :2].transpose(1, 0, 2)
    q_all = jnp.where(h == 0, whole, whole[::-1]).reshape(32, 1, 128)
    prob_grad = jnp.sum(jnp.where(hit, q_all.transpose(0, 2, 1), 0.0), axis=0).astype(BF)
    lead = leader[0]
    is_lead = rank == lead
    is_live = replicas[0][rank] == 1
    lead_mv = lax.dynamic_index_in_dim(mvs, lead, 0, keepdims=False)
    m_new = beta_one * m_old + (1.0 - beta_one) * grad
    v_new = beta_two * v_old + (1.0 - beta_two) * grad * grad
    m_w = jnp.where(is_lead, m_new, beta_one * lead_mv[0].astype(F32) + (1.0 - beta_one) * grad)
    v_w = jnp.where(is_lead, v_new, beta_two * lead_mv[1].astype(F32) + (1.0 - beta_two) * grad * grad)
    m_hat = m_w / (1.0 - beta_one**adam_step)
    v_hat = v_w / (1.0 - beta_two**adam_step)
    w_wide = w_down[0].astype(F32)
    w_new = (w_wide - learn_rate * (m_hat / (jnp.sqrt(v_hat) + adam_eps) + weight_decay * w_wide)).astype(BF)
    new_down = jnp.where(is_live, w_new, w_down[0])[None, None]
    new_one = jnp.where(is_lead, m_new, m_old)[None, None]
    new_two = jnp.where(is_lead, v_new, v_old)[None, None]
    return (token_grad, prob_grad, new_down, new_one, new_two)


def solution(mesh):
    in_specs = (
        P(("dp", "expert"), None),
        P(("dp", "expert"), None),
        P(("dp", "expert"), None),
        P(("dp", "expert"), None),
        P("expert", None, None),
        P("expert", None, None),
        P("dp", "expert", None, None),
        P("dp", "expert", None, None),
        P("expert", None),
        P("expert"),
    )
    out_specs = (
        P(("dp", "expert"), None),
        P(("dp", "expert"), None),
        P("dp", "expert", None, None),
        P("dp", "expert", None, None),
        P("dp", "expert", None, None),
    )
    return jax.shard_map(body, mesh=mesh, in_specs=in_specs, out_specs=out_specs, check_vma=False)
```

```python
import jax
import jax.numpy as jnp
from jax import lax
from jax.experimental import pallas as pl
from jax.experimental.pallas import tpu as pltpu
from jax.sharding import PartitionSpec as P

F32, BF = jnp.float32, jnp.bfloat16
MESH = pl.DeviceIdType.MESH
learn_rate = 0.01
beta_one = 0.9
beta_two = 0.95
adam_eps = 1e-08
weight_decay = 0.1
adam_step = 100


ORDER = ((0, 0), (3, 0), (1, 0), (0, 3), (0, 1), (3, 3), (3, 1), (1, 3), (1, 1), (2, 0), (0, 2), (3, 2), (1, 2), (2, 3), (2, 1), (2, 2))
SLOT = {p: n for n, p in enumerate(ORDER)}


def slot_of(dx, dy):
    return SLOT[dx % 4, dy % 4]


def nt(a, b):
    return lax.dot_general(a, b, (((1,), (1,)), ((), ())), preferred_element_type=F32)


def tn(a, b):
    return lax.dot_general(a, b, (((0,), (0,)), ((), ())), preferred_element_type=F32)


def place():
    dp = lax.axis_index("dp")
    ex = lax.axis_index("expert")
    return dp // 2, dp % 2, ex // 16, (ex // 4) % 4, ex % 4


def greet(peers):
    barrier = pltpu.get_barrier_semaphore()
    for peer in peers:
        pl.semaphore_signal(barrier, inc=1, device_id=peer, device_id_type=MESH)
    pl.semaphore_wait(barrier, len(peers))


def rdma(src, dst, s, r, peer):
    c = pltpu.make_async_remote_copy(src, dst, s, r, device_id=peer, device_id_type=MESH)
    c.start()
    return c


def forward_kernel(tok, grad, pst, wgu, wdn, mold, vold, dout, gfull, qout, mvs,
                   xs, ds, prec, gus, dns, xc, dc, oall, opall, ps, gu_s, g_s, pre_s, hid_s, stage, gacc, mvb,
                   own_sem, w_sem, out_sem, psend, precv, asend, arecv, wsend, wrecv):
    zl, co, h, x, y = place()
    dp = zl * 2 + co
    me = h * 16 + x * 4 + y

    def at(dx, dy):
        return (dp, h * 16 + ((x + dx) % 4) * 4 + (y + dy) % 4)

    sibling = (zl * 2 + 1 - co, me)
    cross = ((1 - zl) * 2 + co, (1 - h) * 16 + x * 4 + y)
    zside = ((1 - zl) * 2 + co, me)
    inputs, outs = (tok, grad), (xs, ds)
    local = [pltpu.make_async_copy(inputs[a], outs[a].at[0], own_sem.at[a]) for a in range(2)]
    local.append(pltpu.make_async_copy(pst.at[x * 4 + y], prec.at[0], own_sem.at[2]))
    mv_in = [pltpu.make_async_copy(mold.at[0, 0], gacc.at[0], w_sem.at[0]), pltpu.make_async_copy(vold.at[0, 0], gacc.at[1], w_sem.at[1])]
    own_w = [pltpu.make_async_copy(wgu.at[0], gus.at[0], w_sem.at[2]), pltpu.make_async_copy(wdn.at[0], dns.at[0], w_sem.at[3])]
    for c in local + mv_in + own_w:
        c.start()
    greet([at(*ORDER[n]) for n in range(1, 16)] + [sibling, cross, zside])

    rows_gu, rows_dn = pl.ds(co * 1024, 1024), pl.ds(co * 192, 192)
    w1 = rdma(wgu.at[0, rows_gu], gus.at[1, rows_gu], wsend.at[0], wrecv.at[0], cross)
    w2 = rdma(wdn.at[0, rows_dn], dns.at[1, rows_dn], wsend.at[1], wrecv.at[1], cross)

    copies = [{}, {}]
    half = (pl.ds(0, 64), pl.ds(64, 64))

    def rel(a, i, j):
        return (i, j) if a == 0 else (j, i)

    def step(a, t, first):
        s = 1 - 2 * t
        return rel(a, s, 0) if first else rel(a, 0, s)

    def sem_at(i, j, first):
        return 0 if first else 1 + i % 4

    def send(a, i, j, first, t, part):
        d = step(a, t, first)
        bx, by = rel(a, i, j)
        src_slot, dst_slot = slot_of(bx, by), slot_of(bx - d[0], by - d[1])
        k = sem_at(i, j, first)
        p = 0 if part is None else 1
        if part is None:
            src = inputs[a] if (bx, by) == (0, 0) else outs[a].at[src_slot]
            dst = outs[a].at[dst_slot]
        else:
            src, dst = outs[a].at[src_slot, half[part]], outs[a].at[dst_slot, half[part]]
        copies[a][k, t, p] = rdma(src, dst, asend.at[a, k, t, p], arecv.at[a, k, t, p], at(*d))

    def send_full(a, i, first):
        for t in range(2):
            send(a, i, 0, first, t, None)

    def pass_on(a, i, first):
        k = sem_at(i, 0, first)
        for t in range(2):
            copies[a][k, t, 0].wait_recv()
            s = 2 * t - 1
            if first:
                send(a, s, 0, True, t, t)
            else:
                send(a, i, s, False, t, t)

    def wait_halves(a, i, first):
        k = sem_at(i, 0, first)
        for t in range(2):
            copies[a][k, t, 1].wait_recv()

    for a in range(2):
        send_full(a, 0, True)
    for a in range(2):
        send_full(a, 0, False)
    pc = []
    for n in range(1, 16):
        dx, dy = ORDER[n]
        pc.append(rdma(pst.at[((x + dx) % 4) * 4 + (y + dy) % 4], prec.at[slot_of(-dx, -dy)], psend.at[n], precv.at[slot_of(-dx, -dy)], at(dx, dy)))
    for c in mv_in:
        c.wait()

    def narrow(t, _):
        rows = pl.ds(pl.multiple_of(t * 64, 64), 64)
        for e in range(2):
            mvb[e, rows] = gacc[e, rows].astype(BF)
        return 0

    lax.fori_loop(0, 6, narrow, 0)
    dmv = mvs.at[dp]
    m1 = rdma(mvb, dmv, wsend.at[2], wrecv.at[2], zside)
    m2 = rdma(mvb, dmv, wsend.at[3], wrecv.at[3], sibling)
    gacc[...] = jnp.zeros_like(gacc)
    oall[...] = jnp.zeros_like(oall)
    opall[...] = jnp.zeros_like(opall)
    qout[...] = jnp.zeros_like(qout)
    for c in local + own_w:
        c.wait()

    before = (lax.broadcasted_iota(jnp.int32, (128, 128), 0) < lax.broadcasted_iota(jnp.int32, (128, 128), 1)).astype(BF)
    slot = lax.broadcasted_iota(jnp.int32, (64, 128), 0).astype(F32)

    def pack(base, j):
        for i in range(2):
            p = prec[base + j * 2 + i]
            on = (p > 0).astype(F32)
            rank = jnp.dot(on.astype(BF), before, preferred_element_type=F32)
            rank = jnp.where(on > 0, rank, -1.0)
            for e in range(2):
                hot = rank[e:e + 1, :] == slot
                oall[j, pl.ds(e * 128 + i * 64, 64), pl.ds(i * 128, 128)] = hot.astype(F32).astype(BF)
                held = jnp.where(hot, p[e:e + 1, :], 0.0)
                opall[pl.ds(e * 128 + i * 64, 64), pl.ds(i * 128, 128)] = held.astype(BF)
                col = jnp.sum(held, axis=1, keepdims=True)
                ps[e, pl.ds(pl.multiple_of(j * 128 + i * 64, 64), 64), :] = jnp.broadcast_to(col, (64, 128))
        rows = pl.ds(pl.multiple_of(j * 128, 128), 128)
        blocks = pl.ds(base + j * 2, 2)
        for o, src, dst in ((oall[j], xs, xc), (opall[...], ds, dc)):
            r = jnp.dot(o, src[blocks].reshape(256, 2048), preferred_element_type=F32).astype(BF)
            dst[0, rows] = r[:128]
            dst[1, rows] = r[128:]

    def expert(e, tiles):
        def tile(t, _):
            rows = pl.ds(pl.multiple_of(t * 256, 256), 256)
            gu_s[...] = jnp.dot(xc[e, rows], gus[e], preferred_element_type=F32)
            g_s[...] = nt(dc[e, rows], dns[e])
            gate, up, g = gu_s[:, :384], gu_s[:, 384:], g_s[...]
            p = ps[e, rows, :1]
            sig = 0.5 * jnp.tanh(0.5 * gate) + 0.5
            silu = gate * sig
            hid = (silu * up).astype(BF)
            q = jnp.sum(hid.astype(F32) * g, axis=1, keepdims=True) / jnp.where(p > 0, p, 1.0)
            hid_s[rows] = hid
            pre_s[:, :384] = (g * up * (sig * (1.0 + gate * (1.0 - sig)))).astype(BF)
            pre_s[:, 384:] = (g * silu).astype(BF)
            ps[e, rows, :] = jnp.broadcast_to(q, (256, 128))
            xc[e, rows] = nt(pre_s[...], gus[e]).astype(BF)
            return 0

        lax.fori_loop(0, tiles, tile, 0)
        n = tiles * 256
        gacc[e] += tn(hid_s[:n], dc[e, :n])

    def out(k):
        return pltpu.make_async_copy(stage.at[k % 2], dout.at[pl.ds(k * 2, 2)], out_sem.at[k % 2])

    def spread(base, j):
        n = base // 2 + j

        @pl.when(n >= 2)
        def _():
            out(n - 2).wait()

        rows = pl.ds(pl.multiple_of(j * 128, 128), 128)
        o = oall[j]
        r = tn(o[:128], xc[0, rows]) + tn(o[128:], xc[1, rows])
        stage[n % 2] = r.astype(BF).reshape(2, 128, 2048)
        out(n).start()
        for i in range(2):
            for e in range(2):
                hot = oall[j, pl.ds(e * 128 + i * 64, 64), pl.ds(i * 128, 128)].astype(F32)
                q = ps[e, pl.ds(pl.multiple_of(j * 128 + i * 64, 64), 64), :]
                qout[base + j * 2 + i, e:e + 1, :] = jnp.sum(hot * q, axis=0, keepdims=True)

    def loop(n, f, base):
        def go(j, _):
            f(base, j)
            return 0
        lax.fori_loop(0, n, go, 0)

    for a in range(2):
        pass_on(a, 0, True)
    for i in (3, 1):
        for a in range(2):
            send_full(a, i, False)
    for a in range(2):
        pass_on(a, 0, False)
    for a in range(2):
        wait_halves(a, 0, True)
    for a in range(2):
        send_full(a, 2, False)
    for c in pc:
        c.wait_recv()
    loop(2, pack, 0)
    for i in (3, 1):
        for a in range(2):
            pass_on(a, i, False)

    def late(j, _):
        pack(0, j + 2)
        return 0

    lax.fori_loop(0, 2, late, 0)
    expert(0, 2)
    w1.wait_recv()
    v1 = rdma(gus.at[1, rows_gu], gus.at[1, rows_gu], wsend.at[4], wrecv.at[4], sibling)
    w2.wait_recv()
    v2 = rdma(dns.at[1, rows_dn], dns.at[1, rows_dn], wsend.at[5], wrecv.at[5], sibling)
    for a in range(2):
        pass_on(a, 2, False)
    v1.wait_recv()
    v2.wait_recv()
    expert(1, 2)
    loop(4, spread, 0)
    m1.wait_recv()
    zdp = (1 - zl) * 2 + co
    m3 = rdma(mvs.at[zdp], mvs.at[zdp], wsend.at[6], wrecv.at[6], sibling)
    for i in (0, 3):
        for a in range(2):
            wait_halves(a, i, False)
    loop(2, pack, 8)
    for e in range(2):
        expert(e, 1)
    loop(2, spread, 8)
    for i in (1, 2):
        for a in range(2):
            wait_halves(a, i, False)
    loop(2, pack, 12)
    for e in range(2):
        expert(e, 1)
    keep = pltpu.make_async_copy(gacc, gfull, own_sem.at[3])
    keep.start()
    loop(2, spread, 12)
    for k in (6, 7):
        out(k).wait()
    keep.wait()
    m2.wait_recv()
    m3.wait_recv()
    for a in range(2):
        for c in copies[a].values():
            c.wait_send()
    for c in [w1, w2, m1, m2, m3, v1, v2] + pc:
        c.wait_send()


def forward(tok, grad, pst, wgu, wdn, mold, vold):
    any_ = pl.BlockSpec(memory_space=pl.ANY)
    vm = pl.BlockSpec(memory_space=pltpu.VMEM)
    sd, dma, V = jax.ShapeDtypeStruct, pltpu.SemaphoreType.DMA, pltpu.VMEM
    return pl.pallas_call(
        forward_kernel,
        name="forward_rows",
        out_shape=(sd((16, 128, 2048), BF), sd((2, 384, 2048), F32), sd((16, 8, 128), F32), sd((4, 2, 384, 2048), BF)),
        in_specs=[any_] * 7,
        out_specs=(any_, any_, vm, any_),
        scratch_shapes=[
            V((16, 128, 2048), BF), V((16, 128, 2048), BF), V((16, 8, 128), F32),
            V((2, 2048, 768), BF), V((2, 384, 2048), BF),
            V((2, 512, 2048), BF), V((2, 512, 2048), BF),
            V((4, 256, 256), BF), V((256, 256), BF), V((2, 512, 128), F32),
            V((256, 768), F32), V((256, 384), F32), V((256, 768), BF), V((512, 384), BF),
            V((2, 2, 128, 2048), BF), V((2, 384, 2048), F32), V((2, 384, 2048), BF),
            dma((4,)), dma((4,)), dma((2,)), dma((16,)), dma((16,)), dma((2, 5, 2, 2)), dma((2, 5, 2, 2)), dma((7,)), dma((7,)),
        ],
        compiler_params=pltpu.CompilerParams(collective_id=0, has_side_effects=True, vmem_limit_bytes=64 * 1024 * 1024 - 65536),
    )(tok, grad, pst, wgu, wdn, mold, vold)


def return_kernel(d, g, q, routes, tout, gfull, pout, dv, relay, full, part, relay2, full2, gv, near, fsend, frecv, osend, orecv, gsum, qrecv,
                  lsem, s1, r1, s2, r2, ws, wr, qs, qr):
    zl, co, h, x, y = place()
    me = x * 4 + y
    dp = zl * 2 + co
    base = h * 16
    sibling = (zl * 2 + 1 - co, base + me)
    cross = ((1 - zl) * 2 + co, (1 - h) * 16 + me)
    zside = ((1 - zl) * 2 + co, base + me)

    def rel(a, i, j):
        return (i, j) if a == 0 else (j, i)

    def spot(a, i, j):
        return slot_of(*rel(a, i, j))

    def at(dx, dy):
        return (dp, base + ((x + dx) % 4) * 4 + (y + dy) % 4)

    mine, other = pl.ds(co * 192, 192), pl.ds((1 - co) * 192, 192)
    loads = [pltpu.make_async_copy(d, dv, lsem.at[0])]
    loads += [pltpu.make_async_copy(g.at[e, mine], gv.at[e], lsem.at[1 + e]) for e in range(2)]
    for c in loads:
        c.start()
    greet([at(*ORDER[n]) for n in range(1, 16)] + [sibling, cross, zside])

    sent = []
    near_in = [[None] * 3 for _ in range(2)]
    for n in range(3):
        for e in (1, 0):
            c = rdma(g.at[e, pl.ds((1 - co) * 192 + n * 64, 64)], near.at[e, pl.ds(n * 64, 64)], ws.at[e, n], wr.at[e, n], sibling)
            near_in[e][n] = c
    order = (2, 1, 3, 0)
    half = (pl.ds(0, 32), pl.ds(32, 32))
    first = {}
    for jj in order:
        for a in range(2):
            far = spot(a, 2, jj)
            for t in range(2):
                peer = at(*rel(a, 1 - 2 * t, 0))
                first[a, jj, t, 0] = rdma(d.at[far, pl.ds(a * 64 + t * 32, 32)], relay.at[a, jj, t], s1.at[a, jj, t, 0], r1.at[a, jj, t, 0], peer)
    for jj in order:
        for a in range(2):
            for t in range(2):
                peer = at(*rel(a, 1 - 2 * t, 0))
                to = spot(a, 1 - 2 * t, jj)
                first[a, jj, t, 1] = rdma(d.at[to, pl.ds(a * 64 + (1 - t) * 32, 32)], full.at[a, jj, t, half[1 - t]], s1.at[a, jj, t, 1], r1.at[a, jj, t, 1], peer)
    qc = [rdma(q.at[n], qrecv.at[me], qs.at[n], qr.at[slot_of(-ORDER[n][0], -ORDER[n][1])], at(*ORDER[n])) for n in range(1, 16)]
    for c in loads:
        c.wait()

    def add_relay(jj, a, t):
        first[a, jj, t, 0].wait_recv()
        to = spot(a, 1 - 2 * t, jj)
        peer = at(*rel(a, 1 - 2 * t, 0))
        relay[a, jj, t] = (relay[a, jj, t].astype(F32) + dv[to, a * 64 + t * 32:a * 64 + t * 32 + 32].astype(F32)).astype(BF)
        first[a, jj, t, 2] = rdma(relay.at[a, jj, t], full.at[a, jj, t, half[t]], s1.at[a, jj, t, 2], r1.at[a, jj, t, 2], peer)

    def foreign(n):
        rows = pl.ds(n * 64, 64)
        near_in[1][n].wait_recv()
        fsend[rows] = (gv[1, rows] + near[1, rows]).astype(BF)
        return rdma(fsend.at[rows], frecv.at[rows], ws.at[2, n], wr.at[2, n], cross)

    def ours(n, f):
        rows = pl.ds(n * 64, 64)
        near_in[0][n].wait_recv()
        f.wait_recv()
        v = gv[0, rows] + near[0, rows] + frecv[rows].astype(F32)
        gsum[rows] = v
        osend[rows] = v.astype(BF)
        return rdma(osend.at[rows], orecv.at[rows], ws.at[3, n], wr.at[3, n], zside)

    def whole(n, o):
        rows = pl.ds(n * 64, 64)
        o.wait_recv()
        gsum[rows] = gsum[rows] + orecv[rows].astype(F32)
        out = pl.ds(co * 192 + n * 64, 64)
        loc = pltpu.make_async_copy(gsum.at[rows], gfull.at[out], lsem.at[3 + n])
        loc.start()
        return loc, rdma(gsum.at[rows], gfull.at[out], ws.at[4, n], wr.at[4, n], sibling)

    second = {}

    def line_sum(jj, a):
        for t in range(2):
            first[a, jj, t, 1].wait_recv()
            first[a, jj, t, 2].wait_recv()
        here = spot(a, 0, jj)
        part[a, jj] = (dv[here, a * 64:a * 64 + 64].astype(F32) + full[a, jj, 0].astype(F32) + full[a, jj, 1].astype(F32)).astype(BF)
        side = [at(*rel(a, 0, 1 - 2 * t)) for t in range(2)]
        if jj == 2:
            for t in range(2):
                second[a, t, 0] = rdma(part.at[a, 2, half[t]], relay2.at[a, t], s2.at[a, t, 0], r2.at[a, t, 0], side[t])
        elif jj != 0:
            t = 0 if jj == 1 else 1
            second[a, t, 1] = rdma(part.at[a, jj, half[1 - t]], full2.at[a, t, half[1 - t]], s2.at[a, t, 1], r2.at[a, t, 1], side[t])
            second[a, t, 0].wait_recv()
            relay2[a, t] = (relay2[a, t].astype(F32) + part[a, jj, t * 32:t * 32 + 32].astype(F32)).astype(BF)
            second[a, t, 2] = rdma(relay2.at[a, t], full2.at[a, t, half[t]], s2.at[a, t, 2], r2.at[a, t, 2], side[t])

    fs, os, gs = [], [], []
    for jj in order:
        for a in range(2):
            for t in range(2):
                add_relay(jj, a, t)
        if jj != 2:
            fs.append(foreign(len(fs)))
    os.append(ours(0, fs[0]))
    for a in range(2):
        line_sum(2, a)
    os.append(ours(1, fs[1]))
    for a in range(2):
        line_sum(1, a)
    os.append(ours(2, fs[2]))
    gs.append(whole(0, os[0]))
    for a in range(2):
        line_sum(3, a)
    gs.append(whole(1, os[1]))
    for a in range(2):
        line_sum(0, a)
    gs.append(whole(2, os[2]))
    for c in qc:
        c.wait_recv()
    qrecv[me] = q[0]
    table = qrecv[...].reshape(128, 128)
    line = lax.broadcasted_iota(jnp.int32, (128, 128), 0)
    place8 = lax.broadcasted_iota(jnp.int32, (8, 128), 0)
    probs_out = jnp.zeros((8, 128), F32)
    for k in range(8):
        e = routes[k:k + 1, :]
        want = (e & 15) * 8 + jnp.where((e >> 4) == h, 0, 1)
        row = jnp.sum(jnp.where(line == want, table, 0.0), axis=0, keepdims=True)
        probs_out = jnp.where(place8 == k, row, probs_out)
    pout[...] = probs_out.astype(BF)
    for a in range(2):
        for t in range(2):
            second[a, t, 1].wait_recv()
            second[a, t, 2].wait_recv()
        tout[a * 64:a * 64 + 64, :] = (part[a, 0].astype(F32) + full2[a, 0].astype(F32) + full2[a, 1].astype(F32)).astype(BF)
    for loc, c in gs:
        loc.wait()
        c.wait_recv()
    for c in list(first.values()) + list(second.values()) + near_in[0] + near_in[1] + fs + os + [c for _, c in gs] + qc:
        c.wait_send()


def give_back(d, g, q, routes):
    any_ = pl.BlockSpec(memory_space=pl.ANY)
    vm = pl.BlockSpec(memory_space=pltpu.VMEM)
    sd = jax.ShapeDtypeStruct
    dma = pltpu.SemaphoreType.DMA
    return pl.pallas_call(
        return_kernel,
        name="return_rows",
        out_shape=(sd((128, 2048), BF), sd((384, 2048), F32), sd((8, 128), BF)),
        in_specs=[any_, any_, vm, vm],
        out_specs=(vm, any_, vm),
        scratch_shapes=[
            pltpu.VMEM((16, 128, 2048), BF),
            pltpu.VMEM((2, 4, 2, 32, 2048), BF), pltpu.VMEM((2, 4, 2, 64, 2048), BF), pltpu.VMEM((2, 4, 64, 2048), BF),
            pltpu.VMEM((2, 2, 32, 2048), BF), pltpu.VMEM((2, 2, 64, 2048), BF),
            pltpu.VMEM((2, 192, 2048), F32), pltpu.VMEM((2, 192, 2048), F32),
            pltpu.VMEM((192, 2048), BF), pltpu.VMEM((192, 2048), BF), pltpu.VMEM((192, 2048), BF), pltpu.VMEM((192, 2048), BF),
            pltpu.VMEM((192, 2048), F32), pltpu.VMEM((16, 8, 128), F32),
            dma((6,)), dma((2, 4, 2, 3)), dma((2, 4, 2, 3)), dma((2, 2, 3)), dma((2, 2, 3)), dma((5, 3)), dma((5, 3)), dma((16,)), dma((16,)),
        ],
        compiler_params=pltpu.CompilerParams(collective_id=1, has_side_effects=True, vmem_limit_bytes=60 * 1024 * 1024),
    )(d, g, q, routes)


def adam_kernel(flags, g, m, v, lead_mv, w, down, one, two):
    is_lead, is_live = flags[1] == 1, flags[2] == 1
    grad, m_old, v_old = g[...], m[0, 0], v[0, 0]
    m_src = jnp.where(is_lead, m_old, lead_mv[0, 0].astype(F32))
    v_src = jnp.where(is_lead, v_old, lead_mv[0, 1].astype(F32))
    m_new = beta_one * m_src + (1.0 - beta_one) * grad
    v_new = beta_two * v_src + (1.0 - beta_two) * grad * grad
    m_hat = m_new / (1.0 - beta_one**adam_step)
    v_hat = v_new / (1.0 - beta_two**adam_step)
    w_wide = w[0].astype(F32)
    w_new = (w_wide - learn_rate * (m_hat / (jnp.sqrt(v_hat) + adam_eps) + weight_decay * w_wide)).astype(BF)
    down[0, 0] = jnp.where(is_live, w_new, w[0])
    one[0, 0] = jnp.where(is_lead, m_new, m_old)
    two[0, 0] = jnp.where(is_lead, v_new, v_old)


def adam(flags, g, m, v, mvs, w):
    rows = 48
    sd = jax.ShapeDtypeStruct
    four = pl.BlockSpec((1, 1, rows, 2048), lambda i, f: (0, 0, i, 0))
    return pl.pallas_call(
        adam_kernel,
        name="adam_rows",
        out_shape=(sd((1, 1, 384, 2048), BF), sd((1, 1, 384, 2048), F32), sd((1, 1, 384, 2048), F32)),
        grid_spec=pltpu.PrefetchScalarGridSpec(
            num_scalar_prefetch=1, grid=(384 // rows,),
            in_specs=[pl.BlockSpec((rows, 2048), lambda i, f: (i, 0)), four, four,
                      pl.BlockSpec((1, 2, rows, 2048), lambda i, f: (f[0], 0, i, 0)),
                      pl.BlockSpec((1, rows, 2048), lambda i, f: (0, i, 0))],
            out_specs=(four, four, four)),
    )(flags, g, m, v, mvs, w)


def body(tokens, out_grad, routes, probs, w_gate_up, w_down, moment_one, moment_two, replicas, leader):
    rank = lax.axis_index("dp")
    ex = lax.axis_index("expert")
    h = ex // 16
    ids = jnp.arange(32, dtype=jnp.int32)
    hit = routes.T[:, None, :] == ids[None, :, None]
    dense = jnp.sum(jnp.where(hit, probs.T.astype(F32)[:, None, :], 0.0), axis=0).reshape(2, 16, 128)
    near = lax.dynamic_index_in_dim(dense, h, 0, keepdims=False)
    far = lax.dynamic_index_in_dim(dense, 1 - h, 0, keepdims=False)
    pst = jnp.pad(jnp.stack([near, far], axis=1), ((0, 0), (0, 6), (0, 0)))
    m_old, v_old = moment_one[0, 0], moment_two[0, 0]
    d, g, q, mvs = forward(tokens, out_grad, pst, w_gate_up, w_down, moment_one, moment_two)
    token_grad, grad, prob_grad = give_back(d, g, q, routes.T)
    lead = leader[0]
    flags = jnp.stack([lead, (rank == lead).astype(jnp.int32), replicas[0][rank]])
    new_down, new_one, new_two = adam(flags, grad, moment_one, moment_two, mvs, w_down)
    return (token_grad, prob_grad.T, new_down, new_one, new_two)


def solution(mesh):
    in_specs = (
        P(("dp", "expert"), None),
        P(("dp", "expert"), None),
        P(("dp", "expert"), None),
        P(("dp", "expert"), None),
        P("expert", None, None),
        P("expert", None, None),
        P("dp", "expert", None, None),
        P("dp", "expert", None, None),
        P("expert", None),
        P("expert"),
    )
    out_specs = (
        P(("dp", "expert"), None),
        P(("dp", "expert"), None),
        P("dp", "expert", None, None),
        P("dp", "expert", None, None),
        P("dp", "expert", None, None),
    )
    return jax.shard_map(body, mesh=mesh, in_specs=in_specs, out_specs=out_specs, check_vma=False)
```

```python
import jax
import jax.numpy as jnp
from jax import lax
from jax.experimental import pallas as pl
from jax.experimental.pallas import tpu as pltpu
from jax.sharding import PartitionSpec as P

F32, BF = jnp.float32, jnp.bfloat16
MESH = pl.DeviceIdType.MESH
learn_rate = 0.01
beta_one = 0.9
beta_two = 0.95
adam_eps = 1e-08
weight_decay = 0.1
adam_step = 100


ORDER = ((0, 0), (3, 0), (1, 0), (0, 3), (0, 1), (3, 3), (3, 1), (1, 3), (1, 1), (2, 0), (0, 2), (3, 2), (1, 2), (2, 3), (2, 1), (2, 2))
SLOT = {p: n for n, p in enumerate(ORDER)}


def slot_of(dx, dy):
    return SLOT[dx % 4, dy % 4]


def nt(a, b):
    return lax.dot_general(a, b, (((1,), (1,)), ((), ())), preferred_element_type=F32)


def tn(a, b):
    return lax.dot_general(a, b, (((0,), (0,)), ((), ())), preferred_element_type=F32)


def place():
    dp = lax.axis_index("dp")
    ex = lax.axis_index("expert")
    return dp // 2, dp % 2, ex // 16, (ex // 4) % 4, ex % 4


def greet(peers):
    barrier = pltpu.get_barrier_semaphore()
    for peer in peers:
        pl.semaphore_signal(barrier, inc=1, device_id=peer, device_id_type=MESH)
    pl.semaphore_wait(barrier, len(peers))


def rdma(src, dst, s, r, peer):
    c = pltpu.make_async_remote_copy(src, dst, s, r, device_id=peer, device_id_type=MESH)
    c.start()
    return c


def layer_kernel(tok, grad, pst, wgu, wdn, mold, vold, routes, tout, gfull, pout, mvs,
                 xs, ds, prec, gus, dns, xc, dc, oall, opall, ps, gu_s, g_s, pre_s, hid_s, gacc, mvb, qout,
                 relay, full, relay2, full2, near, frecv, orecv, qrecv,
                 own_sem, w_sem, psend, precv, asend, arecv, wsend, wrecv, s1, r1, s2, r2, ws, wr, qs, qr):
    zl, co, h, x, y = place()
    dp = zl * 2 + co
    me = h * 16 + x * 4 + y

    def at(dx, dy):
        return (dp, h * 16 + ((x + dx) % 4) * 4 + (y + dy) % 4)

    sibling = (zl * 2 + 1 - co, me)
    cross = ((1 - zl) * 2 + co, (1 - h) * 16 + x * 4 + y)
    zside = ((1 - zl) * 2 + co, me)
    inputs, outs = (tok, grad), (xs, ds)
    local = [pltpu.make_async_copy(inputs[a], outs[a].at[0], own_sem.at[a]) for a in range(2)]
    local.append(pltpu.make_async_copy(pst.at[x * 4 + y], prec.at[0], own_sem.at[2]))
    mv_in = [pltpu.make_async_copy(mold.at[0, 0], gacc.at[0], w_sem.at[0]), pltpu.make_async_copy(vold.at[0, 0], gacc.at[1], w_sem.at[1])]
    own_w = [pltpu.make_async_copy(wgu.at[0], gus.at[0], w_sem.at[2]), pltpu.make_async_copy(wdn.at[0], dns.at[0], w_sem.at[3])]
    for c in local + mv_in + own_w:
        c.start()
    greet([at(*ORDER[n]) for n in range(1, 16)] + [sibling, cross, zside])

    rows_gu, rows_dn = pl.ds(co * 1024, 1024), pl.ds(co * 192, 192)
    w1 = rdma(wgu.at[0, rows_gu], gus.at[1, rows_gu], wsend.at[0], wrecv.at[0], cross)
    w2 = rdma(wdn.at[0, rows_dn], dns.at[1, rows_dn], wsend.at[1], wrecv.at[1], cross)

    copies = [{}, {}]
    readers = {n: [] for n in range(16)}
    half = (pl.ds(0, 64), pl.ds(64, 64))

    def rel(a, i, j):
        return (i, j) if a == 0 else (j, i)

    def step(a, t, first):
        s = 1 - 2 * t
        return rel(a, s, 0) if first else rel(a, 0, s)

    def sem_at(i, j, first):
        return 0 if first else 1 + i % 4

    def send(a, i, j, first, t, part):
        d = step(a, t, first)
        bx, by = rel(a, i, j)
        src_slot, dst_slot = slot_of(bx, by), slot_of(bx - d[0], by - d[1])
        k = sem_at(i, j, first)
        p = 0 if part is None else 1
        if part is None:
            src = inputs[a] if (bx, by) == (0, 0) else outs[a].at[src_slot]
            dst = outs[a].at[dst_slot]
        else:
            src, dst = outs[a].at[src_slot, half[part]], outs[a].at[dst_slot, half[part]]
        copies[a][k, t, p] = rdma(src, dst, asend.at[a, k, t, p], arecv.at[a, k, t, p], at(*d))
        if a == 0 and (part is not None or (bx, by) != (0, 0)):
            readers[src_slot].append(copies[a][k, t, p])

    def send_full(a, i, first):
        for t in range(2):
            send(a, i, 0, first, t, None)

    def pass_on(a, i, first):
        k = sem_at(i, 0, first)
        for t in range(2):
            copies[a][k, t, 0].wait_recv()
            s = 2 * t - 1
            if first:
                send(a, s, 0, True, t, t)
            else:
                send(a, i, s, False, t, t)

    def wait_halves(a, i, first):
        k = sem_at(i, 0, first)
        for t in range(2):
            copies[a][k, t, 1].wait_recv()

    for a in range(2):
        send_full(a, 0, True)
    for a in range(2):
        send_full(a, 0, False)
    pc = []
    for n in range(1, 16):
        dx, dy = ORDER[n]
        pc.append(rdma(pst.at[((x + dx) % 4) * 4 + (y + dy) % 4], prec.at[slot_of(-dx, -dy)], psend.at[n], precv.at[slot_of(-dx, -dy)], at(dx, dy)))
    for c in mv_in:
        c.wait()

    def narrow(t, _):
        rows = pl.ds(pl.multiple_of(t * 64, 64), 64)
        for e in range(2):
            mvb[e, rows] = gacc[e, rows].astype(BF)
        return 0

    lax.fori_loop(0, 6, narrow, 0)
    dmv = mvs.at[dp]
    m1 = rdma(mvb, dmv, wsend.at[2], wrecv.at[2], zside)
    m2 = rdma(mvb, dmv, wsend.at[3], wrecv.at[3], sibling)
    gacc[...] = jnp.zeros_like(gacc)
    oall[...] = jnp.zeros_like(oall)
    opall[...] = jnp.zeros_like(opall)
    qout[...] = jnp.zeros_like(qout)
    for c in local + own_w:
        c.wait()

    before = (lax.broadcasted_iota(jnp.int32, (128, 128), 0) < lax.broadcasted_iota(jnp.int32, (128, 128), 1)).astype(BF)
    slot = lax.broadcasted_iota(jnp.int32, (64, 128), 0).astype(F32)

    def pack(base, j):
        for i in range(2):
            p = prec[base + j * 2 + i]
            on = (p > 0).astype(F32)
            rank = jnp.dot(on.astype(BF), before, preferred_element_type=F32)
            rank = jnp.where(on > 0, rank, -1.0)
            for e in range(2):
                hot = rank[e:e + 1, :] == slot
                oall[j, pl.ds(e * 128 + i * 64, 64), pl.ds(i * 128, 128)] = hot.astype(F32).astype(BF)
                held = jnp.where(hot, p[e:e + 1, :], 0.0)
                opall[pl.ds(e * 128 + i * 64, 64), pl.ds(i * 128, 128)] = held.astype(BF)
                col = jnp.sum(held, axis=1, keepdims=True)
                ps[e, pl.ds(pl.multiple_of(j * 128 + i * 64, 64), 64), :] = jnp.broadcast_to(col, (64, 128))
        rows = pl.ds(pl.multiple_of(j * 128, 128), 128)
        blocks = pl.ds(base + j * 2, 2)
        for o, src, dst in ((oall[j], xs, xc), (opall[...], ds, dc)):
            r = jnp.dot(o, src[blocks].reshape(256, 2048), preferred_element_type=F32).astype(BF)
            dst[0, rows] = r[:128]
            dst[1, rows] = r[128:]

    def expert(e, tiles):
        def tile(t, _):
            rows = pl.ds(pl.multiple_of(t * 256, 256), 256)
            gu_s[...] = jnp.dot(xc[e, rows], gus[e], preferred_element_type=F32)
            g_s[...] = nt(dc[e, rows], dns[e])
            gate, up, g = gu_s[:, :384], gu_s[:, 384:], g_s[...]
            p = ps[e, rows, :1]
            sig = 0.5 * jnp.tanh(0.5 * gate) + 0.5
            silu = gate * sig
            hid = (silu * up).astype(BF)
            q = jnp.sum(hid.astype(F32) * g, axis=1, keepdims=True) / jnp.where(p > 0, p, 1.0)
            hid_s[rows] = hid
            pre_s[:, :384] = (g * up * (sig * (1.0 + gate * (1.0 - sig)))).astype(BF)
            pre_s[:, 384:] = (g * silu).astype(BF)
            ps[e, rows, :] = jnp.broadcast_to(q, (256, 128))
            xc[e, rows] = nt(pre_s[...], gus[e]).astype(BF)
            return 0

        lax.fori_loop(0, tiles, tile, 0)
        n = tiles * 256
        gacc[e] += tn(hid_s[:n], dc[e, :n])

    def spread(base, j):
        rows = pl.ds(pl.multiple_of(j * 128, 128), 128)
        o = oall[j]
        r = tn(o[:128], xc[0, rows]) + tn(o[128:], xc[1, rows])
        xs[pl.ds(base + j * 2, 2)] = r.astype(BF).reshape(2, 128, 2048)
        for i in range(2):
            for e in range(2):
                hot = oall[j, pl.ds(e * 128 + i * 64, 64), pl.ds(i * 128, 128)].astype(F32)
                q = ps[e, pl.ds(pl.multiple_of(j * 128 + i * 64, 64), 64), :]
                qout[base + j * 2 + i, e:e + 1, :] = jnp.sum(hot * q, axis=0, keepdims=True)

    def loop(n, f, base):
        def go(j, _):
            f(base, j)
            return 0
        lax.fori_loop(0, n, go, 0)

    order = (2, 1, 3, 0)
    quarter = (pl.ds(0, 32), pl.ds(32, 32))
    first, second = {}, {}
    qc = []

    def spot(a, i, j):
        return slot_of(*rel(a, i, j))

    def give(lo, hi):
        for kind in range(2):
            for jj in order:
                for a in range(2):
                    for t in range(2):
                        peer = at(*rel(a, 1 - 2 * t, 0))
                        b = spot(a, 2 if kind == 0 else 1 - 2 * t, jj)
                        if not lo <= b < hi:
                            continue
                        if kind == 0:
                            src, dst = xs.at[b, pl.ds(a * 64 + t * 32, 32)], relay.at[a, jj, t]
                        else:
                            src, dst = xs.at[b, pl.ds(a * 64 + (1 - t) * 32, 32)], full.at[a, jj, t, quarter[1 - t]]
                        first[a, jj, t, kind] = rdma(src, dst, s1.at[a, jj, t, kind], r1.at[a, jj, t, kind], peer)
        for n in range(max(lo, 1), hi):
            dx, dy = ORDER[n]
            back = slot_of(-dx, -dy)
            qc.append(rdma(qout.at[n], qrecv.at[x * 4 + y], qs.at[n], qr.at[back], at(dx, dy)))

    def spread_all(base, pairs):
        for n in range(base, base + 2 * pairs):
            for c in readers[n]:
                c.wait_send()
        loop(pairs, spread, base)
        give(base, base + 2 * pairs)

    def add_relay(jj, a):
        for t in range(2):
            first[a, jj, t, 0].wait_recv()
            to = spot(a, 1 - 2 * t, jj)
            lo = a * 64 + t * 32
            relay[a, jj, t] = (relay[a, jj, t].astype(F32) + xs[to, lo:lo + 32].astype(F32)).astype(BF)
            first[a, jj, t, 2] = rdma(relay.at[a, jj, t], full.at[a, jj, t, quarter[t]], s1.at[a, jj, t, 2], r1.at[a, jj, t, 2], at(*rel(a, 1 - 2 * t, 0)))

    def part(a, jj):
        return xc.at[a, pl.ds(jj * 64, 64)]

    def line_sum(jj, a):
        for t in range(2):
            first[a, jj, t, 1].wait_recv()
            first[a, jj, t, 2].wait_recv()
        here = spot(a, 0, jj)
        mine = part(a, jj)
        mine[...] = (xs[here, a * 64:a * 64 + 64].astype(F32) + full[a, jj, 0].astype(F32) + full[a, jj, 1].astype(F32)).astype(BF)
        side = [at(*rel(a, 0, 1 - 2 * t)) for t in range(2)]
        if jj == 2:
            for t in range(2):
                second[a, t, 0] = rdma(mine.at[quarter[t]], relay2.at[a, t], s2.at[a, t, 0], r2.at[a, t, 0], side[t])
        elif jj != 0:
            t = 0 if jj == 1 else 1
            second[a, t, 1] = rdma(mine.at[quarter[1 - t]], full2.at[a, t, quarter[1 - t]], s2.at[a, t, 1], r2.at[a, t, 1], side[t])
            second[a, t, 0].wait_recv()
            relay2[a, t] = (relay2[a, t].astype(F32) + mine[t * 32:t * 32 + 32].astype(F32)).astype(BF)
            second[a, t, 2] = rdma(relay2.at[a, t], full2.at[a, t, quarter[t]], s2.at[a, t, 2], r2.at[a, t, 2], side[t])

    near_in = [[None] * 3 for _ in range(2)]

    def halves():
        for n in range(3):
            for e in (1, 0):
                near_in[e][n] = rdma(gacc.at[e, pl.ds((1 - co) * 192 + n * 64, 64)], near.at[e, pl.ds(n * 64, 64)], ws.at[e, n], wr.at[e, n], sibling)

    def rows_of(n):
        return pl.ds(pl.multiple_of(co * 192 + n * 64, 64), 64), pl.ds(n * 64, 64)

    def foreign(n):
        mine, rows = rows_of(n)
        near_in[1][n].wait_recv()
        mvb[0, rows] = (gacc[1, mine] + near[1, rows]).astype(BF)
        return rdma(mvb.at[0, rows], frecv.at[rows], ws.at[2, n], wr.at[2, n], cross)

    def ours(n, f):
        mine, rows = rows_of(n)
        near_in[0][n].wait_recv()
        f.wait_recv()
        v = gacc[0, mine] + near[0, rows] + frecv[rows].astype(F32)
        gacc[0, mine] = v
        mvb[1, rows] = v.astype(BF)
        return rdma(mvb.at[1, rows], orecv.at[rows], ws.at[3, n], wr.at[3, n], zside)

    def whole(n, o):
        mine, rows = rows_of(n)
        o.wait_recv()
        gacc[0, mine] = gacc[0, mine] + orecv[rows].astype(F32)
        loc = pltpu.make_async_copy(gacc.at[0, mine], gfull.at[mine], w_sem.at[n])
        loc.start()
        return loc, rdma(gacc.at[0, mine], gfull.at[mine], ws.at[4, n], wr.at[4, n], sibling)

    for a in range(2):
        pass_on(a, 0, True)
    for i in (3, 1):
        for a in range(2):
            send_full(a, i, False)
    for a in range(2):
        pass_on(a, 0, False)
    for a in range(2):
        wait_halves(a, 0, True)
    for a in range(2):
        send_full(a, 2, False)
    for c in pc:
        c.wait_recv()
    loop(2, pack, 0)
    for i in (3, 1):
        for a in range(2):
            pass_on(a, i, False)

    def late(j, _):
        pack(0, j + 2)
        return 0

    lax.fori_loop(0, 2, late, 0)
    expert(0, 2)
    w1.wait_recv()
    v1 = rdma(gus.at[1, rows_gu], gus.at[1, rows_gu], wsend.at[4], wrecv.at[4], sibling)
    w2.wait_recv()
    v2 = rdma(dns.at[1, rows_dn], dns.at[1, rows_dn], wsend.at[5], wrecv.at[5], sibling)
    for a in range(2):
        pass_on(a, 2, False)
    v1.wait_recv()
    v2.wait_recv()
    expert(1, 2)
    spread_all(0, 4)
    m1.wait_recv()
    zdp = (1 - zl) * 2 + co
    m3 = rdma(mvs.at[zdp], mvs.at[zdp], wsend.at[6], wrecv.at[6], sibling)
    for i in (0, 3):
        for a in range(2):
            wait_halves(a, i, False)
    loop(2, pack, 8)
    for e in range(2):
        expert(e, 1)
    spread_all(8, 2)
    for i in (1, 2):
        for a in range(2):
            wait_halves(a, i, False)
    loop(2, pack, 12)
    expert(0, 1)
    early = ((0, 0), (0, 1), (3, 1))
    for jj, a in early:
        add_relay(jj, a)
    expert(1, 1)
    for c in (m1, m2):
        c.wait_send()
    halves()
    spread_all(12, 2)
    fs, os, gs = [], [], []
    for jj in order:
        for a in range(2):
            if (jj, a) not in early:
                add_relay(jj, a)
        if jj != 0:
            fs.append(foreign(len(fs)))
    os.append(ours(0, fs[0]))
    for a in range(2):
        line_sum(2, a)
    os.append(ours(1, fs[1]))
    for a in range(2):
        line_sum(1, a)
    os.append(ours(2, fs[2]))
    gs.append(whole(0, os[0]))
    for a in range(2):
        line_sum(3, a)
    gs.append(whole(1, os[1]))
    for a in range(2):
        line_sum(0, a)
    gs.append(whole(2, os[2]))
    for c in qc:
        c.wait_recv()
    qrecv[x * 4 + y] = qout[0]
    table = qrecv[...].reshape(128, 128)
    line = lax.broadcasted_iota(jnp.int32, (128, 128), 0)
    place8 = lax.broadcasted_iota(jnp.int32, (8, 128), 0)
    probs_out = jnp.zeros((8, 128), F32)
    for k in range(8):
        e = routes[k:k + 1, :]
        want = (e & 15) * 8 + jnp.where((e >> 4) == h, 0, 1)
        row = jnp.sum(jnp.where(line == want, table, 0.0), axis=0, keepdims=True)
        probs_out = jnp.where(place8 == k, row, probs_out)
    pout[...] = probs_out.astype(BF)
    for a in range(2):
        for t in range(2):
            second[a, t, 1].wait_recv()
            second[a, t, 2].wait_recv()
        tout[a * 64:a * 64 + 64, :] = (part(a, 0)[...].astype(F32) + full2[a, 0].astype(F32) + full2[a, 1].astype(F32)).astype(BF)
    for loc, c in gs:
        loc.wait()
        c.wait_recv()
    m2.wait_recv()
    m3.wait_recv()
    done = [c for n in range(16) for c in readers[n]]
    for a in range(2):
        for c in copies[a].values():
            if not any(c is d for d in done):
                c.wait_send()
    for c in list(first.values()) + list(second.values()) + near_in[0] + near_in[1] + fs + os + [c for _, c in gs] + qc:
        c.wait_send()
    for c in [w1, w2, m3, v1, v2] + pc:
        c.wait_send()


def layer(tok, grad, pst, wgu, wdn, mold, vold, routes):
    any_ = pl.BlockSpec(memory_space=pl.ANY)
    vm = pl.BlockSpec(memory_space=pltpu.VMEM)
    sd, dma, V = jax.ShapeDtypeStruct, pltpu.SemaphoreType.DMA, pltpu.VMEM
    return pl.pallas_call(
        layer_kernel,
        name="layer_rows",
        out_shape=(sd((128, 2048), BF), sd((384, 2048), F32), sd((8, 128), BF), sd((4, 2, 384, 2048), BF)),
        in_specs=[any_] * 7 + [vm],
        out_specs=(vm, any_, vm, any_),
        scratch_shapes=[
            V((16, 128, 2048), BF), V((16, 128, 2048), BF), V((16, 8, 128), F32),
            V((2, 2048, 768), BF), V((2, 384, 2048), BF),
            V((2, 512, 2048), BF), V((2, 512, 2048), BF),
            V((4, 256, 256), BF), V((256, 256), BF), V((2, 512, 128), F32),
            V((256, 768), F32), V((256, 384), F32), V((256, 768), BF), V((512, 384), BF),
            V((2, 384, 2048), F32), V((2, 384, 2048), BF), V((16, 8, 128), F32),
            V((2, 4, 2, 32, 2048), BF), V((2, 4, 2, 64, 2048), BF), V((2, 2, 32, 2048), BF), V((2, 2, 64, 2048), BF),
            V((2, 192, 2048), F32), V((192, 2048), BF), V((192, 2048), BF), V((16, 8, 128), F32),
            dma((3,)), dma((4,)), dma((16,)), dma((16,)), dma((2, 5, 2, 2)), dma((2, 5, 2, 2)), dma((7,)), dma((7,)),
            dma((2, 4, 2, 3)), dma((2, 4, 2, 3)), dma((2, 2, 3)), dma((2, 2, 3)), dma((5, 3)), dma((5, 3)), dma((16,)), dma((16,)),
        ],
        compiler_params=pltpu.CompilerParams(collective_id=0, has_side_effects=True, vmem_limit_bytes=67043328),
    )(tok, grad, pst, wgu, wdn, mold, vold, routes)


def adam_kernel(flags, g, m, v, mvs, w, down, one, two, gv, mb, vb, lb, wb, sem, osem):
    rows, steps = 64, 6
    is_lead, is_live = flags[1] == 1, flags[2] == 1

    def loads(i):
        r = pl.ds(i * rows, rows)
        return (pltpu.make_async_copy(g.at[r], gv.at[r], sem.at[0, i]),
                pltpu.make_async_copy(m.at[0, 0, r], mb.at[r], sem.at[1, i]),
                pltpu.make_async_copy(v.at[0, 0, r], vb.at[r], sem.at[2, i]),
                pltpu.make_async_copy(mvs.at[flags[0], :, r], lb.at[:, r], sem.at[3, i]),
                pltpu.make_async_copy(w.at[0, r], wb.at[r], sem.at[4, i]))

    def stores(i):
        r = pl.ds(i * rows, rows)
        return (pltpu.make_async_copy(wb.at[r], down.at[0, 0, r], osem.at[0, i]),
                pltpu.make_async_copy(mb.at[r], one.at[0, 0, r], osem.at[1, i]),
                pltpu.make_async_copy(vb.at[r], two.at[0, 0, r], osem.at[2, i]))

    for i in range(steps):
        for c in loads(i):
            c.start()

    def step(i, _):
        for c in loads(i):
            c.wait()

        def part(t, _):
            r = pl.ds(pl.multiple_of(i * rows + t * 16, 16), 16)
            grad, m_old, v_old, w_old = gv[r], mb[r], vb[r], wb[r]
            m_src = jnp.where(is_lead, m_old, lb[0, r].astype(F32))
            v_src = jnp.where(is_lead, v_old, lb[1, r].astype(F32))
            m_new = beta_one * m_src + (1.0 - beta_one) * grad
            v_new = beta_two * v_src + (1.0 - beta_two) * grad * grad
            m_hat = m_new * (1.0 / (1.0 - beta_one**adam_step))
            v_hat = v_new * (1.0 / (1.0 - beta_two**adam_step))
            w_wide = w_old.astype(F32)
            w_new = (w_wide - learn_rate * (m_hat / (jnp.sqrt(v_hat) + adam_eps) + weight_decay * w_wide)).astype(BF)
            wb[r] = jnp.where(is_live, w_new, w_old)
            mb[r] = jnp.where(is_lead, m_new, m_old)
            vb[r] = jnp.where(is_lead, v_new, v_old)
            return 0

        lax.fori_loop(0, rows // 16, part, 0)
        for c in stores(i):
            c.start()
        return 0

    lax.fori_loop(0, steps, step, 0)
    for i in range(steps):
        for c in stores(i):
            c.wait()


def adam(flags, g, m, v, mvs, w):
    sd, V = jax.ShapeDtypeStruct, pltpu.VMEM
    any_ = pl.BlockSpec(memory_space=pl.ANY)
    return pl.pallas_call(
        adam_kernel,
        name="adam_rows",
        out_shape=(sd((1, 1, 384, 2048), BF), sd((1, 1, 384, 2048), F32), sd((1, 1, 384, 2048), F32)),
        in_specs=[pl.BlockSpec(memory_space=pltpu.SMEM)] + [any_] * 5,
        out_specs=(any_,) * 3,
        scratch_shapes=[V((384, 2048), F32), V((384, 2048), F32), V((384, 2048), F32), V((2, 384, 2048), BF), V((384, 2048), BF),
                        pltpu.SemaphoreType.DMA((5, 6)), pltpu.SemaphoreType.DMA((3, 6))],
    )(flags, g, m, v, mvs, w)


def body(tokens, out_grad, routes, probs, w_gate_up, w_down, moment_one, moment_two, replicas, leader):
    rank = lax.axis_index("dp")
    ex = lax.axis_index("expert")
    h = ex // 16
    ids = jnp.arange(32, dtype=jnp.int32)
    hit = routes.T[:, None, :] == ids[None, :, None]
    dense = jnp.sum(jnp.where(hit, probs.T.astype(F32)[:, None, :], 0.0), axis=0).reshape(2, 16, 128)
    near = lax.dynamic_index_in_dim(dense, h, 0, keepdims=False)
    far = lax.dynamic_index_in_dim(dense, 1 - h, 0, keepdims=False)
    pst = jnp.pad(jnp.stack([near, far], axis=1), ((0, 0), (0, 6), (0, 0)))
    m_old, v_old = moment_one[0, 0], moment_two[0, 0]
    token_grad, grad, prob_grad, mvs = layer(tokens, out_grad, pst, w_gate_up, w_down, moment_one, moment_two, routes.T)
    lead = leader[0]
    flags = jnp.stack([lead, (rank == lead).astype(jnp.int32), replicas[0][rank]])
    new_down, new_one, new_two = adam(flags, grad, moment_one, moment_two, mvs, w_down)
    return (token_grad, prob_grad.T, new_down, new_one, new_two)


def solution(mesh):
    in_specs = (
        P(("dp", "expert"), None),
        P(("dp", "expert"), None),
        P(("dp", "expert"), None),
        P(("dp", "expert"), None),
        P("expert", None, None),
        P("expert", None, None),
        P("dp", "expert", None, None),
        P("dp", "expert", None, None),
        P("expert", None),
        P("expert"),
    )
    out_specs = (
        P(("dp", "expert"), None),
        P(("dp", "expert"), None),
        P("dp", "expert", None, None),
        P("dp", "expert", None, None),
        P("dp", "expert", None, None),
    )
    return jax.shard_map(body, mesh=mesh, in_specs=in_specs, out_specs=out_specs, check_vma=False)
```

```python
import jax
import jax.numpy as jnp
from jax import lax
from jax.experimental import pallas as pl
from jax.experimental.pallas import tpu as pltpu
from jax.sharding import PartitionSpec as P

F32, BF = jnp.float32, jnp.bfloat16
MESH = pl.DeviceIdType.MESH
learn_rate = 0.01
beta_one = 0.9
beta_two = 0.95
adam_eps = 1e-08
weight_decay = 0.1
adam_step = 100


ORDER = ((0, 0), (3, 0), (1, 0), (0, 3), (0, 1), (3, 3), (3, 1), (1, 3), (1, 1), (2, 0), (0, 2), (3, 2), (1, 2), (2, 3), (2, 1), (2, 2))
SLOT = {p: n for n, p in enumerate(ORDER)}


def slot_of(dx, dy):
    return SLOT[dx % 4, dy % 4]


def nt(a, b):
    return lax.dot_general(a, b, (((1,), (1,)), ((), ())), preferred_element_type=F32)


def tn(a, b):
    return lax.dot_general(a, b, (((0,), (0,)), ((), ())), preferred_element_type=F32)


def place():
    dp = lax.axis_index("dp")
    ex = lax.axis_index("expert")
    return dp // 2, dp % 2, ex // 16, (ex // 4) % 4, ex % 4


def greet(peers):
    barrier = pltpu.get_barrier_semaphore()
    for peer in peers:
        pl.semaphore_signal(barrier, inc=1, device_id=peer, device_id_type=MESH)
    pl.semaphore_wait(barrier, len(peers))


def rdma(src, dst, s, r, peer):
    c = pltpu.make_async_remote_copy(src, dst, s, r, device_id=peer, device_id_type=MESH)
    c.start()
    return c


def layer_kernel(tok, grad, wgu, wdn, mold, vold, routes, probs, tout, gfull, pout, mvs,
                 xs, ds, prec, pst, gus, dns, xc, dc, oall, opall, ps, gu_s, g_s, pre_s, hid_s, gacc, mvb, qout,
                 relay, full, relay2, full2, near, frecv, orecv, qrecv,
                 own_sem, w_sem, psend, precv, asend, arecv, wsend, wrecv, s1, r1, s2, r2, ws, wr, qs, qr):
    zl, co, h, x, y = place()
    dp = zl * 2 + co
    me = h * 16 + x * 4 + y

    def at(dx, dy):
        return (dp, h * 16 + ((x + dx) % 4) * 4 + (y + dy) % 4)

    sibling = (zl * 2 + 1 - co, me)
    cross = ((1 - zl) * 2 + co, (1 - h) * 16 + x * 4 + y)
    zside = ((1 - zl) * 2 + co, me)
    inputs, outs = (tok, grad), (xs, ds)
    local = [pltpu.make_async_copy(inputs[a], outs[a].at[0], own_sem.at[a]) for a in range(2)]
    mv_in = [pltpu.make_async_copy(mold.at[0, 0], gacc.at[0], w_sem.at[0]), pltpu.make_async_copy(vold.at[0, 0], gacc.at[1], w_sem.at[1])]
    own_w = [pltpu.make_async_copy(wgu.at[0], gus.at[0], w_sem.at[2]), pltpu.make_async_copy(wdn.at[0], dns.at[0], w_sem.at[3])]
    for c in local + mv_in + own_w:
        c.start()
    line = lax.broadcasted_iota(jnp.int32, (128, 128), 0)

    def line_of(k):
        e = routes[k:k + 1, :]
        return (e & 15) * 8 + jnp.where((e >> 4) == h, 0, 1)

    dense = jnp.zeros((128, 128), F32)
    for k in range(8):
        dense = jnp.where(line == line_of(k), probs[k:k + 1, :].astype(F32), dense)
    pst[...] = dense.reshape(16, 8, 128)
    prec[0] = pst[x * 4 + y]
    greet([at(*ORDER[n]) for n in range(1, 16)] + [sibling, cross, zside])

    rows_gu, rows_dn = pl.ds(co * 1024, 1024), pl.ds(co * 192, 192)
    w1 = rdma(wgu.at[0, rows_gu], gus.at[1, rows_gu], wsend.at[0], wrecv.at[0], cross)
    w2 = rdma(wdn.at[0, rows_dn], dns.at[1, rows_dn], wsend.at[1], wrecv.at[1], cross)

    copies = [{}, {}]
    readers = {n: [] for n in range(16)}
    half = (pl.ds(0, 64), pl.ds(64, 64))

    def rel(a, i, j):
        return (i, j) if a == 0 else (j, i)

    def step(a, t, first):
        s = 1 - 2 * t
        return rel(a, s, 0) if first else rel(a, 0, s)

    def sem_at(i, j, first):
        return 0 if first else 1 + i % 4

    def send(a, i, j, first, t, part):
        d = step(a, t, first)
        bx, by = rel(a, i, j)
        src_slot, dst_slot = slot_of(bx, by), slot_of(bx - d[0], by - d[1])
        k = sem_at(i, j, first)
        p = 0 if part is None else 1
        if part is None:
            src = inputs[a] if (bx, by) == (0, 0) else outs[a].at[src_slot]
            dst = outs[a].at[dst_slot]
        else:
            src, dst = outs[a].at[src_slot, half[part]], outs[a].at[dst_slot, half[part]]
        copies[a][k, t, p] = rdma(src, dst, asend.at[a, k, t, p], arecv.at[a, k, t, p], at(*d))
        if a == 0 and (part is not None or (bx, by) != (0, 0)):
            readers[src_slot].append(copies[a][k, t, p])

    def send_full(a, i, first):
        for t in range(2):
            send(a, i, 0, first, t, None)

    def pass_on(a, i, first):
        k = sem_at(i, 0, first)
        for t in range(2):
            copies[a][k, t, 0].wait_recv()
            s = 2 * t - 1
            if first:
                send(a, s, 0, True, t, t)
            else:
                send(a, i, s, False, t, t)

    def wait_halves(a, i, first):
        k = sem_at(i, 0, first)
        for t in range(2):
            copies[a][k, t, 1].wait_recv()

    for a in range(2):
        send_full(a, 0, True)
    for a in range(2):
        send_full(a, 0, False)
    pc = []
    for n in range(1, 16):
        dx, dy = ORDER[n]
        pc.append(rdma(pst.at[((x + dx) % 4) * 4 + (y + dy) % 4], prec.at[slot_of(-dx, -dy)], psend.at[n], precv.at[slot_of(-dx, -dy)], at(dx, dy)))
    for c in mv_in:
        c.wait()

    def narrow(t, _):
        rows = pl.ds(pl.multiple_of(t * 64, 64), 64)
        for e in range(2):
            mvb[e, rows] = gacc[e, rows].astype(BF)
        return 0

    lax.fori_loop(0, 6, narrow, 0)
    dmv = mvs.at[dp]
    m1 = rdma(mvb, dmv, wsend.at[2], wrecv.at[2], zside)
    m2 = rdma(mvb, dmv, wsend.at[3], wrecv.at[3], sibling)
    gacc[...] = jnp.zeros_like(gacc)
    oall[...] = jnp.zeros_like(oall)
    opall[...] = jnp.zeros_like(opall)
    qout[...] = jnp.zeros_like(qout)
    for c in local + own_w:
        c.wait()

    before = (lax.broadcasted_iota(jnp.int32, (128, 128), 0) < lax.broadcasted_iota(jnp.int32, (128, 128), 1)).astype(BF)
    slot = lax.broadcasted_iota(jnp.int32, (64, 128), 0).astype(F32)

    def pack(base, j):
        for i in range(2):
            p = prec[base + j * 2 + i]
            on = (p > 0).astype(F32)
            rank = jnp.dot(on.astype(BF), before, preferred_element_type=F32)
            rank = jnp.where(on > 0, rank, -1.0)
            for e in range(2):
                hot = rank[e:e + 1, :] == slot
                oall[j, pl.ds(e * 128 + i * 64, 64), pl.ds(i * 128, 128)] = hot.astype(F32).astype(BF)
                held = jnp.where(hot, p[e:e + 1, :], 0.0)
                opall[pl.ds(e * 128 + i * 64, 64), pl.ds(i * 128, 128)] = held.astype(BF)
                col = jnp.sum(held, axis=1, keepdims=True)
                ps[e, pl.ds(pl.multiple_of(j * 128 + i * 64, 64), 64), :] = jnp.broadcast_to(col, (64, 128))
        rows = pl.ds(pl.multiple_of(j * 128, 128), 128)
        blocks = pl.ds(base + j * 2, 2)
        for o, src, dst in ((oall[j], xs, xc), (opall[...], ds, dc)):
            r = jnp.dot(o, src[blocks].reshape(256, 2048), preferred_element_type=F32).astype(BF)
            dst[0, rows] = r[:128]
            dst[1, rows] = r[128:]

    def expert(e, tiles):
        def tile(t, _):
            rows = pl.ds(pl.multiple_of(t * 256, 256), 256)
            gu_s[...] = jnp.dot(xc[e, rows], gus[e], preferred_element_type=F32)
            g_s[...] = nt(dc[e, rows], dns[e])
            gate, up, g = gu_s[:, :384], gu_s[:, 384:], g_s[...]
            p = ps[e, rows, :1]
            sig = 0.5 * jnp.tanh(0.5 * gate) + 0.5
            silu = gate * sig
            hid = (silu * up).astype(BF)
            q = jnp.sum(hid.astype(F32) * g, axis=1, keepdims=True) / jnp.where(p > 0, p, 1.0)
            hid_s[rows] = hid
            pre_s[:, :384] = (g * up * (sig * (1.0 + gate * (1.0 - sig)))).astype(BF)
            pre_s[:, 384:] = (g * silu).astype(BF)
            ps[e, rows, :] = jnp.broadcast_to(q, (256, 128))
            xc[e, rows] = nt(pre_s[...], gus[e]).astype(BF)
            return 0

        lax.fori_loop(0, tiles, tile, 0)
        n = tiles * 256
        gacc[e] += tn(hid_s[:n], dc[e, :n])

    def spread(base, j):
        rows = pl.ds(pl.multiple_of(j * 128, 128), 128)
        o = oall[j]
        r = tn(o[:128], xc[0, rows]) + tn(o[128:], xc[1, rows])
        xs[pl.ds(base + j * 2, 2)] = r.astype(BF).reshape(2, 128, 2048)
        for i in range(2):
            for e in range(2):
                hot = oall[j, pl.ds(e * 128 + i * 64, 64), pl.ds(i * 128, 128)].astype(F32)
                q = ps[e, pl.ds(pl.multiple_of(j * 128 + i * 64, 64), 64), :]
                qout[base + j * 2 + i, e:e + 1, :] = jnp.sum(hot * q, axis=0, keepdims=True)

    def loop(n, f, base):
        def go(j, _):
            f(base, j)
            return 0
        lax.fori_loop(0, n, go, 0)

    order = (2, 1, 3, 0)
    quarter = (pl.ds(0, 32), pl.ds(32, 32))
    first, second = {}, {}
    qc = []

    def spot(a, i, j):
        return slot_of(*rel(a, i, j))

    def give(lo, hi):
        for kind in range(2):
            for jj in order:
                for a in range(2):
                    for t in range(2):
                        peer = at(*rel(a, 1 - 2 * t, 0))
                        b = spot(a, 2 if kind == 0 else 1 - 2 * t, jj)
                        if not lo <= b < hi:
                            continue
                        if kind == 0:
                            src, dst = xs.at[b, pl.ds(a * 64 + t * 32, 32)], relay.at[a, jj, t]
                        else:
                            src, dst = xs.at[b, pl.ds(a * 64 + (1 - t) * 32, 32)], full.at[a, jj, t, quarter[1 - t]]
                        first[a, jj, t, kind] = rdma(src, dst, s1.at[a, jj, t, kind], r1.at[a, jj, t, kind], peer)
        for n in range(max(lo, 1), hi):
            dx, dy = ORDER[n]
            back = slot_of(-dx, -dy)
            qc.append(rdma(qout.at[n], qrecv.at[x * 4 + y], qs.at[n], qr.at[back], at(dx, dy)))

    def spread_all(base, pairs):
        for n in range(base, base + 2 * pairs):
            for c in readers[n]:
                c.wait_send()
        loop(pairs, spread, base)
        give(base, base + 2 * pairs)

    def add_relay(jj, a):
        for t in range(2):
            first[a, jj, t, 0].wait_recv()
            to = spot(a, 1 - 2 * t, jj)
            lo = a * 64 + t * 32
            relay[a, jj, t] = (relay[a, jj, t].astype(F32) + xs[to, lo:lo + 32].astype(F32)).astype(BF)
            first[a, jj, t, 2] = rdma(relay.at[a, jj, t], full.at[a, jj, t, quarter[t]], s1.at[a, jj, t, 2], r1.at[a, jj, t, 2], at(*rel(a, 1 - 2 * t, 0)))

    def part(a, jj):
        return xc.at[a, pl.ds(jj * 64, 64)]

    def line_sum(jj, a):
        for t in range(2):
            first[a, jj, t, 1].wait_recv()
            first[a, jj, t, 2].wait_recv()
        here = spot(a, 0, jj)
        mine = part(a, jj)
        mine[...] = (xs[here, a * 64:a * 64 + 64].astype(F32) + full[a, jj, 0].astype(F32) + full[a, jj, 1].astype(F32)).astype(BF)
        side = [at(*rel(a, 0, 1 - 2 * t)) for t in range(2)]
        if jj == 2:
            for t in range(2):
                second[a, t, 0] = rdma(mine.at[quarter[t]], relay2.at[a, t], s2.at[a, t, 0], r2.at[a, t, 0], side[t])
        elif jj != 0:
            t = 0 if jj == 1 else 1
            second[a, t, 1] = rdma(mine.at[quarter[1 - t]], full2.at[a, t, quarter[1 - t]], s2.at[a, t, 1], r2.at[a, t, 1], side[t])
            second[a, t, 0].wait_recv()
            relay2[a, t] = (relay2[a, t].astype(F32) + mine[t * 32:t * 32 + 32].astype(F32)).astype(BF)
            second[a, t, 2] = rdma(relay2.at[a, t], full2.at[a, t, quarter[t]], s2.at[a, t, 2], r2.at[a, t, 2], side[t])

    near_in = [[None] * 3 for _ in range(2)]

    def halves(e):
        for n in range(3):
            near_in[e][n] = rdma(gacc.at[e, pl.ds((1 - co) * 192 + n * 64, 64)], near.at[e, pl.ds(n * 64, 64)], ws.at[e, n], wr.at[e, n], sibling)

    def rows_of(n):
        return pl.ds(pl.multiple_of(co * 192 + n * 64, 64), 64), pl.ds(n * 64, 64)

    def foreign(n):
        mine, rows = rows_of(n)
        near_in[1][n].wait_recv()
        mvb[0, rows] = (gacc[1, mine] + near[1, rows]).astype(BF)
        return rdma(mvb.at[0, rows], frecv.at[rows], ws.at[2, n], wr.at[2, n], cross)

    def ours(n, f):
        mine, rows = rows_of(n)
        near_in[0][n].wait_recv()
        f.wait_recv()
        v = gacc[0, mine] + near[0, rows] + frecv[rows].astype(F32)
        gacc[0, mine] = v
        mvb[1, rows] = v.astype(BF)
        return rdma(mvb.at[1, rows], orecv.at[rows], ws.at[3, n], wr.at[3, n], zside)

    def whole(n, o):
        mine, rows = rows_of(n)
        o.wait_recv()
        gacc[0, mine] = gacc[0, mine] + orecv[rows].astype(F32)
        loc = pltpu.make_async_copy(gacc.at[0, mine], gfull.at[mine], w_sem.at[n])
        loc.start()
        return loc, rdma(gacc.at[0, mine], gfull.at[mine], ws.at[4, n], wr.at[4, n], sibling)

    for a in range(2):
        pass_on(a, 0, True)
    for i in (3, 1):
        for a in range(2):
            send_full(a, i, False)
    for a in range(2):
        pass_on(a, 0, False)
    for a in range(2):
        wait_halves(a, 0, True)
    for a in range(2):
        send_full(a, 2, False)
    for c in pc:
        c.wait_recv()
    loop(2, pack, 0)
    for i in (3, 1):
        for a in range(2):
            pass_on(a, i, False)

    def late(j, _):
        pack(0, j + 2)
        return 0

    lax.fori_loop(0, 2, late, 0)
    expert(0, 2)
    w1.wait_recv()
    v1 = rdma(gus.at[1, rows_gu], gus.at[1, rows_gu], wsend.at[4], wrecv.at[4], sibling)
    w2.wait_recv()
    v2 = rdma(dns.at[1, rows_dn], dns.at[1, rows_dn], wsend.at[5], wrecv.at[5], sibling)
    for a in range(2):
        pass_on(a, 2, False)
    v1.wait_recv()
    v2.wait_recv()
    expert(1, 2)
    spread_all(0, 4)
    m1.wait_recv()
    zdp = (1 - zl) * 2 + co
    m3 = rdma(mvs.at[zdp], mvs.at[zdp], wsend.at[6], wrecv.at[6], sibling)
    for i in (0, 3):
        for a in range(2):
            wait_halves(a, i, False)
    loop(2, pack, 8)
    for e in range(2):
        expert(e, 1)
    spread_all(8, 2)
    for i in (1, 2):
        for a in range(2):
            wait_halves(a, i, False)
    loop(2, pack, 12)
    for c in (m1, m2):
        c.wait_send()
    expert(1, 1)
    halves(1)
    for jj, a in ((0, 0), (0, 1), (3, 1)):
        add_relay(jj, a)
    expert(0, 1)
    halves(0)
    spread_all(12, 2)
    fs = [foreign(n) for n in range(3)]
    os, gs = [], []
    for jj, a in ((2, 1), (2, 0), (1, 1), (1, 0)):
        add_relay(jj, a)
    os.append(ours(0, fs[0]))
    add_relay(3, 0)
    line_sum(2, 1)
    os.append(ours(1, fs[1]))
    line_sum(2, 0)
    line_sum(1, 1)
    line_sum(3, 1)
    gs.append(whole(0, os[0]))
    line_sum(1, 0)
    os.append(ours(2, fs[2]))
    line_sum(3, 0)
    gs.append(whole(1, os[1]))
    for a in range(2):
        line_sum(0, a)
    gs.append(whole(2, os[2]))
    for c in qc:
        c.wait_recv()
    qrecv[x * 4 + y] = qout[0]
    table = qrecv[...].reshape(128, 128)
    place8 = lax.broadcasted_iota(jnp.int32, (8, 128), 0)
    probs_out = jnp.zeros((8, 128), F32)
    for k in range(8):
        row = jnp.sum(jnp.where(line == line_of(k), table, 0.0), axis=0, keepdims=True)
        probs_out = jnp.where(place8 == k, row, probs_out)
    pout[...] = probs_out.astype(BF)
    for a in range(2):
        for t in range(2):
            second[a, t, 1].wait_recv()
            second[a, t, 2].wait_recv()
        tout[a * 64:a * 64 + 64, :] = (part(a, 0)[...].astype(F32) + full2[a, 0].astype(F32) + full2[a, 1].astype(F32)).astype(BF)
    for loc, c in gs:
        loc.wait()
        c.wait_recv()
    m2.wait_recv()
    m3.wait_recv()
    done = [c for n in range(16) for c in readers[n]]
    for a in range(2):
        for c in copies[a].values():
            if not any(c is d for d in done):
                c.wait_send()
    for c in list(first.values()) + list(second.values()) + near_in[0] + near_in[1] + fs + os + [c for _, c in gs] + qc:
        c.wait_send()
    for c in [w1, w2, m3, v1, v2] + pc:
        c.wait_send()


def layer(tok, grad, wgu, wdn, mold, vold, routes, probs):
    any_ = pl.BlockSpec(memory_space=pl.ANY)
    vm = pl.BlockSpec(memory_space=pltpu.VMEM)
    sd, dma, V = jax.ShapeDtypeStruct, pltpu.SemaphoreType.DMA, pltpu.VMEM
    return pl.pallas_call(
        layer_kernel,
        name="layer_rows",
        out_shape=(sd((128, 2048), BF), sd((384, 2048), F32), sd((8, 128), BF), sd((4, 2, 384, 2048), BF)),
        in_specs=[any_] * 6 + [vm, vm],
        out_specs=(vm, any_, vm, any_),
        scratch_shapes=[
            V((16, 128, 2048), BF), V((16, 128, 2048), BF), V((16, 8, 128), F32), V((16, 8, 128), F32),
            V((2, 2048, 768), BF), V((2, 384, 2048), BF),
            V((2, 512, 2048), BF), V((2, 512, 2048), BF),
            V((4, 256, 256), BF), V((256, 256), BF), V((2, 512, 128), F32),
            V((256, 768), F32), V((256, 384), F32), V((256, 768), BF), V((512, 384), BF),
            V((2, 384, 2048), F32), V((2, 384, 2048), BF), V((16, 8, 128), F32),
            V((2, 4, 2, 32, 2048), BF), V((2, 4, 2, 64, 2048), BF), V((2, 2, 32, 2048), BF), V((2, 2, 64, 2048), BF),
            V((2, 192, 2048), F32), V((192, 2048), BF), V((192, 2048), BF), V((16, 8, 128), F32),
            dma((3,)), dma((4,)), dma((16,)), dma((16,)), dma((2, 5, 2, 2)), dma((2, 5, 2, 2)), dma((7,)), dma((7,)),
            dma((2, 4, 2, 3)), dma((2, 4, 2, 3)), dma((2, 2, 3)), dma((2, 2, 3)), dma((5, 3)), dma((5, 3)), dma((16,)), dma((16,)),
        ],
        compiler_params=pltpu.CompilerParams(collective_id=0, has_side_effects=True, vmem_limit_bytes=67043328),
    )(tok, grad, wgu, wdn, mold, vold, routes, probs)


def adam_kernel(leader, replicas, g, m, v, mvs, w, tg, pg, down, one, two, tg_out, pg_out, gv, mb, vb, lb, wb, tb, sem, osem, tsem):
    rows, steps = 64, 6
    rank = lax.axis_index("dp")
    lead = leader[0]
    is_lead, is_live = lead == rank, replicas[0, rank] == 1

    def loads(i):
        r = pl.ds(i * rows, rows)
        return (pltpu.make_async_copy(g.at[r], gv.at[r], sem.at[0, i]),
                pltpu.make_async_copy(m.at[0, 0, r], mb.at[r], sem.at[1, i]),
                pltpu.make_async_copy(v.at[0, 0, r], vb.at[r], sem.at[2, i]),
                pltpu.make_async_copy(mvs.at[lead, :, r], lb.at[:, r], sem.at[3, i]),
                pltpu.make_async_copy(w.at[0, r], wb.at[r], sem.at[4, i]))

    def stores(i):
        r = pl.ds(i * rows, rows)
        return (pltpu.make_async_copy(wb.at[r], down.at[0, 0, r], osem.at[0, i]),
                pltpu.make_async_copy(mb.at[r], one.at[0, 0, r], osem.at[1, i]),
                pltpu.make_async_copy(vb.at[r], two.at[0, 0, r], osem.at[2, i]))

    t_in, t_out = pltpu.make_async_copy(tg, tb, tsem), pltpu.make_async_copy(tb, tg_out, tsem)
    for i in range(steps):
        for c in loads(i):
            c.start()
    t_in.start()
    pg_out[...] = pg[...]

    def step(i, _):
        for c in loads(i):
            c.wait()

        def part(t, _):
            r = pl.ds(pl.multiple_of(i * rows + t * 16, 16), 16)
            grad, m_old, v_old, w_old = gv[r], mb[r], vb[r], wb[r]
            m_src = jnp.where(is_lead, m_old, lb[0, r].astype(F32))
            v_src = jnp.where(is_lead, v_old, lb[1, r].astype(F32))
            m_new = beta_one * m_src + (1.0 - beta_one) * grad
            v_new = beta_two * v_src + (1.0 - beta_two) * grad * grad
            m_hat = m_new * (1.0 / (1.0 - beta_one**adam_step))
            v_hat = v_new * (1.0 / (1.0 - beta_two**adam_step))
            w_wide = w_old.astype(F32)
            w_new = (w_wide - learn_rate * (m_hat / (jnp.sqrt(v_hat) + adam_eps) + weight_decay * w_wide)).astype(BF)
            wb[r] = jnp.where(is_live, w_new, w_old)
            mb[r] = jnp.where(is_lead, m_new, m_old)
            vb[r] = jnp.where(is_lead, v_new, v_old)
            return 0

        lax.fori_loop(0, rows // 16, part, 0)
        for c in stores(i):
            c.start()
        return 0

    lax.fori_loop(0, steps, step, 0)
    t_in.wait()
    t_out.start()
    t_out.wait()
    for i in range(steps):
        for c in stores(i):
            c.wait()


def adam(leader, replicas, g, m, v, mvs, w, tg, pg):
    sd, V = jax.ShapeDtypeStruct, pltpu.VMEM
    any_ = pl.BlockSpec(memory_space=pl.ANY)
    return pl.pallas_call(
        adam_kernel,
        name="adam_rows",
        out_shape=(sd((1, 1, 384, 2048), BF), sd((1, 1, 384, 2048), F32), sd((1, 1, 384, 2048), F32), sd((128, 2048), BF), sd((8, 128), BF)),
        in_specs=[pl.BlockSpec(memory_space=pltpu.SMEM)] * 2 + [any_] * 6 + [pl.BlockSpec(memory_space=pltpu.VMEM)],
        out_specs=(any_,) * 4 + (pl.BlockSpec(memory_space=pltpu.VMEM),),
        scratch_shapes=[V((384, 2048), F32), V((384, 2048), F32), V((384, 2048), F32), V((2, 384, 2048), BF), V((384, 2048), BF), V((128, 2048), BF),
                        pltpu.SemaphoreType.DMA((5, 6)), pltpu.SemaphoreType.DMA((3, 6)), pltpu.SemaphoreType.DMA],
    )(leader, replicas, g, m, v, mvs, w, tg, pg)


def body(tokens, out_grad, routes, probs, w_gate_up, w_down, moment_one, moment_two, replicas, leader):
    token_grad, grad, prob_grad, mvs = layer(tokens, out_grad, w_gate_up, w_down, moment_one, moment_two, routes.T, probs.T)
    new_down, new_one, new_two, token_grad, prob_grad = adam(leader, replicas, grad, moment_one, moment_two, mvs, w_down, token_grad, prob_grad)
    return (token_grad, prob_grad.T, new_down, new_one, new_two)


def solution(mesh):
    in_specs = (
        P(("dp", "expert"), None),
        P(("dp", "expert"), None),
        P(("dp", "expert"), None),
        P(("dp", "expert"), None),
        P("expert", None, None),
        P("expert", None, None),
        P("dp", "expert", None, None),
        P("dp", "expert", None, None),
        P("expert", None),
        P("expert"),
    )
    out_specs = (
        P(("dp", "expert"), None),
        P(("dp", "expert"), None),
        P("dp", "expert", None, None),
        P("dp", "expert", None, None),
        P("dp", "expert", None, None),
    )
    return jax.shard_map(body, mesh=mesh, in_specs=in_specs, out_specs=out_specs, check_vma=False)
```

```python
import jax
import jax.numpy as jnp
from jax import lax
from jax.experimental import pallas as pl
from jax.experimental.pallas import tpu as pltpu
from jax.sharding import PartitionSpec as P

F32, BF = jnp.float32, jnp.bfloat16
MESH = pl.DeviceIdType.MESH
learn_rate = 0.01
beta_one = 0.9
beta_two = 0.95
adam_eps = 1e-08
weight_decay = 0.1
adam_step = 100


ORDER = ((0, 0), (3, 0), (1, 0), (0, 3), (0, 1), (3, 3), (3, 1), (1, 3), (1, 1), (2, 0), (0, 2), (3, 2), (1, 2), (2, 3), (2, 1), (2, 2))
SLOT = {p: n for n, p in enumerate(ORDER)}


def slot_of(dx, dy):
    return SLOT[dx % 4, dy % 4]


def nt(a, b):
    return lax.dot_general(a, b, (((1,), (1,)), ((), ())), preferred_element_type=F32)


def tn(a, b):
    return lax.dot_general(a, b, (((0,), (0,)), ((), ())), preferred_element_type=F32)


def place():
    dp = lax.axis_index("dp")
    ex = lax.axis_index("expert")
    return dp // 2, dp % 2, ex // 16, (ex // 4) % 4, ex % 4


def greet(peers):
    barrier = pltpu.get_barrier_semaphore()
    for peer in peers:
        pl.semaphore_signal(barrier, inc=1, device_id=peer, device_id_type=MESH)
    pl.semaphore_wait(barrier, len(peers))


def rdma(src, dst, s, r, peer):
    c = pltpu.make_async_remote_copy(src, dst, s, r, device_id=peer, device_id_type=MESH)
    c.start()
    return c


def layer_kernel(tok, grad, wgu, wdn, mold, vold, routes, probs, tout, gfull, pout, mvs,
                 xs, ds, prec, pst, gus, dns, xc, dc, oall, opall, ps, gu_s, g_s, pre_s, hid_s, gacc, qout,
                 dv, relay, full, relay2, full2, near, frecv, orecv, qrecv,
                 own_sem, w_sem, psend, precv, asend, arecv, wsend, wrecv, s1, r1, s2, r2, ws, wr, qs, qr):
    zl, co, h, x, y = place()
    dp = zl * 2 + co
    me = h * 16 + x * 4 + y

    def at(dx, dy):
        return (dp, h * 16 + ((x + dx) % 4) * 4 + (y + dy) % 4)

    sibling = (zl * 2 + 1 - co, me)
    cross = ((1 - zl) * 2 + co, (1 - h) * 16 + x * 4 + y)
    zside = ((1 - zl) * 2 + co, me)
    inputs, outs = (tok, grad), (xs, ds)
    local = [pltpu.make_async_copy(inputs[a], outs[a].at[0], own_sem.at[a]) for a in range(2)]
    mv_in = [pltpu.make_async_copy(mold.at[0, 0], gacc.at[0], w_sem.at[0]), pltpu.make_async_copy(vold.at[0, 0], gacc.at[1], w_sem.at[1])]
    own_w = [pltpu.make_async_copy(wgu.at[0], gus.at[0], w_sem.at[2]), pltpu.make_async_copy(wdn.at[0], dns.at[0], w_sem.at[3])]
    for c in local + mv_in + own_w:
        c.start()
    greet([at(*ORDER[n]) for n in range(1, 16)] + [sibling, cross, zside])

    rows_gu, rows_dn = pl.ds(co * 1024, 1024), pl.ds(co * 192, 192)
    w1 = rdma(wgu.at[0, rows_gu], gus.at[1, rows_gu], wsend.at[0], wrecv.at[0], cross)
    w2 = rdma(wdn.at[0, rows_dn], dns.at[1, rows_dn], wsend.at[1], wrecv.at[1], cross)

    copies = [{}, {}]
    readers = {n: [] for n in range(16)}
    half = (pl.ds(0, 64), pl.ds(64, 64))

    def rel(a, i, j):
        return (i, j) if a == 0 else (j, i)

    def step(a, t, first):
        s = 1 - 2 * t
        return rel(a, s, 0) if first else rel(a, 0, s)

    def sem_at(i, j, first):
        return 0 if first else 1 + i % 4

    def send(a, i, j, first, t, part):
        d = step(a, t, first)
        bx, by = rel(a, i, j)
        src_slot, dst_slot = slot_of(bx, by), slot_of(bx - d[0], by - d[1])
        k = sem_at(i, j, first)
        p = 0 if part is None else 1
        if part is None:
            src = inputs[a] if (bx, by) == (0, 0) else outs[a].at[src_slot]
            dst = outs[a].at[dst_slot]
        else:
            src, dst = outs[a].at[src_slot, half[part]], outs[a].at[dst_slot, half[part]]
        copies[a][k, t, p] = rdma(src, dst, asend.at[a, k, t, p], arecv.at[a, k, t, p], at(*d))
        if a == 0 and (part is not None or (bx, by) != (0, 0)):
            readers[src_slot].append(copies[a][k, t, p])

    def send_full(a, i, first):
        for t in range(2):
            send(a, i, 0, first, t, None)

    def pass_on(a, i, first):
        k = sem_at(i, 0, first)
        for t in range(2):
            copies[a][k, t, 0].wait_recv()
            s = 2 * t - 1
            if first:
                send(a, s, 0, True, t, t)
            else:
                send(a, i, s, False, t, t)

    def wait_halves(a, i, first):
        k = sem_at(i, 0, first)
        for t in range(2):
            copies[a][k, t, 1].wait_recv()

    for a in range(2):
        send_full(a, 0, True)
    for a in range(2):
        send_full(a, 0, False)
    line = lax.broadcasted_iota(jnp.int32, (128, 128), 0)

    def line_of(k):
        e = routes[k:k + 1, :]
        return (e & 15) * 8 + jnp.where((e >> 4) == h, 0, 1)

    dense = jnp.zeros((128, 128), F32)
    for k in range(8):
        dense = jnp.where(line == line_of(k), probs[k:k + 1, :].astype(F32), dense)
    pst[...] = dense.reshape(16, 8, 128)
    prec[0] = pst[x * 4 + y]
    for c in mv_in:
        c.wait()

    def narrow(t, _):
        rows = pl.ds(pl.multiple_of(t * 64, 64), 64)
        for e in range(2):
            dv[e, rows] = gacc[e, rows].astype(BF)
        return 0

    lax.fori_loop(0, 6, narrow, 0)
    pc = []
    for n in range(1, 16):
        dx, dy = ORDER[n]
        pc.append(rdma(pst.at[((x + dx) % 4) * 4 + (y + dy) % 4], prec.at[slot_of(-dx, -dy)], psend.at[n], precv.at[slot_of(-dx, -dy)], at(dx, dy)))
    dmv = mvs.at[dp]
    m1 = rdma(dv.at[:, pl.ds(0, 384)], dmv, wsend.at[2], wrecv.at[2], zside)
    m2 = rdma(dv.at[:, pl.ds(0, 384)], dmv, wsend.at[3], wrecv.at[3], sibling)
    gacc[...] = jnp.zeros_like(gacc)
    oall[...] = jnp.zeros_like(oall)
    opall[...] = jnp.zeros_like(opall)
    qout[...] = jnp.zeros_like(qout)
    for c in local + own_w:
        c.wait()

    before = (lax.broadcasted_iota(jnp.int32, (128, 128), 0) < lax.broadcasted_iota(jnp.int32, (128, 128), 1)).astype(BF)
    slot = lax.broadcasted_iota(jnp.int32, (64, 128), 0).astype(F32)

    def pack(base, j):
        for i in range(2):
            p = prec[base + j * 2 + i]
            on = (p > 0).astype(F32)
            rank = jnp.dot(on.astype(BF), before, preferred_element_type=F32)
            rank = jnp.where(on > 0, rank, -1.0)
            for e in range(2):
                hot = rank[e:e + 1, :] == slot
                oall[j, pl.ds(e * 128 + i * 64, 64), pl.ds(i * 128, 128)] = hot.astype(F32).astype(BF)
                held = jnp.where(hot, p[e:e + 1, :], 0.0)
                opall[pl.ds(e * 128 + i * 64, 64), pl.ds(i * 128, 128)] = held.astype(BF)
                col = jnp.sum(held, axis=1, keepdims=True)
                ps[e, pl.ds(pl.multiple_of(j * 128 + i * 64, 64), 64), :] = jnp.broadcast_to(col, (64, 128))
        rows = pl.ds(pl.multiple_of(j * 128, 128), 128)
        blocks = pl.ds(base + j * 2, 2)
        for o, src, dst in ((oall[j], xs, xc), (opall[...], ds, dc)):
            r = jnp.dot(o, src[blocks].reshape(256, 2048), preferred_element_type=F32).astype(BF)
            dst[0, rows] = r[:128]
            dst[1, rows] = r[128:]

    def expert(e, tiles):
        def tile(t, _):
            rows = pl.ds(pl.multiple_of(t * 256, 256), 256)
            gu_s[...] = jnp.dot(xc[e, rows], gus[e], preferred_element_type=F32)
            g_s[...] = nt(dc[e, rows], dns[e])
            gate, up, g = gu_s[:, :384], gu_s[:, 384:], g_s[...]
            p = ps[e, rows, :1]
            sig = 0.5 * jnp.tanh(0.5 * gate) + 0.5
            silu = gate * sig
            hid = (silu * up).astype(BF)
            q = jnp.sum(hid.astype(F32) * g, axis=1, keepdims=True) / jnp.where(p > 0, p, 1.0)
            hid_s[rows] = hid
            pre_s[:, :384] = (g * up * (sig * (1.0 + gate * (1.0 - sig)))).astype(BF)
            pre_s[:, 384:] = (g * silu).astype(BF)
            ps[e, rows, :] = jnp.broadcast_to(q, (256, 128))
            xc[e, rows] = nt(pre_s[...], gus[e]).astype(BF)
            return 0

        lax.fori_loop(0, tiles, tile, 0)
        n = tiles * 256
        gacc[e] += tn(hid_s[:n], dc[e, :n])

    def spread(base, j):
        rows = pl.ds(pl.multiple_of(j * 128, 128), 128)
        o = oall[j]
        r = tn(o[:128], xc[0, rows]) + tn(o[128:], xc[1, rows])
        if base == 0:
            dv[j // 2, pl.ds(pl.multiple_of(j % 2 * 256, 256), 256)] = r.astype(BF)
        else:
            xs[pl.ds(base + j * 2, 2)] = r.astype(BF).reshape(2, 128, 2048)
        for i in range(2):
            for e in range(2):
                hot = oall[j, pl.ds(e * 128 + i * 64, 64), pl.ds(i * 128, 128)].astype(F32)
                q = ps[e, pl.ds(pl.multiple_of(j * 128 + i * 64, 64), 64), :]
                qout[base + j * 2 + i, e:e + 1, :] = jnp.sum(hot * q, axis=0, keepdims=True)

    def loop(n, f, base):
        def go(j, _):
            f(base, j)
            return 0
        lax.fori_loop(0, n, go, 0)

    order = (2, 1, 3, 0)
    quarter = (pl.ds(0, 32), pl.ds(32, 32))
    first, second = {}, {}
    qc = []

    def spot(a, i, j):
        return slot_of(*rel(a, i, j))

    def sums(n):
        return dv.at[n // 4, pl.ds(n % 4 * 128, 128)] if n < 8 else xs.at[n]

    def give(lo, hi):
        for kind in range(2):
            for jj in order:
                for a in range(2):
                    for t in range(2):
                        peer = at(*rel(a, 1 - 2 * t, 0))
                        b = spot(a, 2 if kind == 0 else 1 - 2 * t, jj)
                        if not lo <= b < hi:
                            continue
                        if kind == 0:
                            src, dst = sums(b).at[pl.ds(a * 64 + t * 32, 32)], relay.at[a, jj, t]
                        else:
                            src, dst = sums(b).at[pl.ds(a * 64 + (1 - t) * 32, 32)], full.at[a, jj, t, quarter[1 - t]]
                        first[a, jj, t, kind] = rdma(src, dst, s1.at[a, jj, t, kind], r1.at[a, jj, t, kind], peer)
        for n in range(max(lo, 1), hi):
            dx, dy = ORDER[n]
            back = slot_of(-dx, -dy)
            qc.append(rdma(qout.at[n], qrecv.at[x * 4 + y], qs.at[n], qr.at[back], at(dx, dy)))

    def spread_all(base, pairs):
        for n in range(max(base, 8), base + 2 * pairs):
            for c in readers[n]:
                c.wait_send()
        loop(pairs, spread, base)
        give(base, base + 2 * pairs)

    def add_relay(jj, a):
        for t in range(2):
            first[a, jj, t, 0].wait_recv()
            to = spot(a, 1 - 2 * t, jj)
            lo = a * 64 + t * 32
            relay[a, jj, t] = (relay[a, jj, t].astype(F32) + sums(to)[lo:lo + 32].astype(F32)).astype(BF)
            first[a, jj, t, 2] = rdma(relay.at[a, jj, t], full.at[a, jj, t, quarter[t]], s1.at[a, jj, t, 2], r1.at[a, jj, t, 2], at(*rel(a, 1 - 2 * t, 0)))

    def part(a, jj):
        return xc.at[a, pl.ds(jj * 64, 64)]

    def line_sum(jj, a):
        for t in range(2):
            first[a, jj, t, 1].wait_recv()
            first[a, jj, t, 2].wait_recv()
        here = spot(a, 0, jj)
        mine = part(a, jj)
        mine[...] = (sums(here)[a * 64:a * 64 + 64].astype(F32) + full[a, jj, 0].astype(F32) + full[a, jj, 1].astype(F32)).astype(BF)
        side = [at(*rel(a, 0, 1 - 2 * t)) for t in range(2)]
        if jj == 2:
            for t in range(2):
                second[a, t, 0] = rdma(mine.at[quarter[t]], relay2.at[a, t], s2.at[a, t, 0], r2.at[a, t, 0], side[t])
        elif jj != 0:
            t = 0 if jj == 1 else 1
            second[a, t, 1] = rdma(mine.at[quarter[1 - t]], full2.at[a, t, quarter[1 - t]], s2.at[a, t, 1], r2.at[a, t, 1], side[t])
            second[a, t, 0].wait_recv()
            relay2[a, t] = (relay2[a, t].astype(F32) + mine[t * 32:t * 32 + 32].astype(F32)).astype(BF)
            second[a, t, 2] = rdma(relay2.at[a, t], full2.at[a, t, quarter[t]], s2.at[a, t, 2], r2.at[a, t, 2], side[t])

    near_in = [[None] * 3 for _ in range(2)]

    def halves(e):
        for n in range(3):
            near_in[e][n] = rdma(gacc.at[e, pl.ds((1 - co) * 192 + n * 64, 64)], near.at[e, pl.ds(n * 64, 64)], ws.at[e, n], wr.at[e, n], sibling)

    def rows_of(n):
        return pl.ds(pl.multiple_of(co * 192 + n * 64, 64), 64), pl.ds(n * 64, 64)

    def foreign(n):
        mine, rows = rows_of(n)
        near_in[1][n].wait_recv()
        xc[0, pl.ds(256 + n * 64, 64)] = (gacc[1, mine] + near[1, rows]).astype(BF)
        return rdma(xc.at[0, pl.ds(256 + n * 64, 64)], frecv.at[rows], ws.at[2, n], wr.at[2, n], cross)

    def ours(n, f):
        mine, rows = rows_of(n)
        near_in[0][n].wait_recv()
        f.wait_recv()
        v = gacc[0, mine] + near[0, rows] + frecv[rows].astype(F32)
        gacc[0, mine] = v
        xc[1, pl.ds(256 + n * 64, 64)] = v.astype(BF)
        return rdma(xc.at[1, pl.ds(256 + n * 64, 64)], orecv.at[rows], ws.at[3, n], wr.at[3, n], zside)

    def whole(n, o):
        mine, rows = rows_of(n)
        o.wait_recv()
        gacc[0, mine] = gacc[0, mine] + orecv[rows].astype(F32)
        loc = pltpu.make_async_copy(gacc.at[0, mine], gfull.at[mine], w_sem.at[n])
        loc.start()
        return loc, rdma(gacc.at[0, mine], gfull.at[mine], ws.at[4, n], wr.at[4, n], sibling)

    for a in range(2):
        pass_on(a, 0, True)
    for i in (3, 1):
        for a in range(2):
            send_full(a, i, False)
    for a in range(2):
        pass_on(a, 0, False)
    for a in range(2):
        wait_halves(a, 0, True)
    for a in range(2):
        send_full(a, 2, False)
    for c in pc:
        c.wait_recv()
    loop(2, pack, 0)
    for i in (3, 1):
        for a in range(2):
            pass_on(a, i, False)

    def late(j, _):
        pack(0, j + 2)
        return 0

    lax.fori_loop(0, 2, late, 0)
    w1.wait_recv()
    v1 = rdma(gus.at[1, rows_gu], gus.at[1, rows_gu], wsend.at[4], wrecv.at[4], sibling)
    w2.wait_recv()
    v2 = rdma(dns.at[1, rows_dn], dns.at[1, rows_dn], wsend.at[5], wrecv.at[5], sibling)
    expert(0, 2)
    v1.wait_recv()
    v2.wait_recv()
    expert(1, 2)
    for a in range(2):
        pass_on(a, 2, False)
    for c in (m1, m2):
        c.wait_send()
    spread_all(0, 4)
    m1.wait_recv()
    zdp = (1 - zl) * 2 + co
    m3 = rdma(mvs.at[zdp], mvs.at[zdp], wsend.at[6], wrecv.at[6], sibling)
    for i in (0, 3):
        for a in range(2):
            wait_halves(a, i, False)
    loop(2, pack, 8)
    for e in range(2):
        expert(e, 1)
    spread_all(8, 2)
    for i in (1, 2):
        for a in range(2):
            wait_halves(a, i, False)
    loop(2, pack, 12)
    expert(1, 1)
    halves(1)
    for jj, a in ((0, 0), (0, 1), (3, 1)):
        add_relay(jj, a)
    expert(0, 1)
    halves(0)
    spread_all(12, 2)
    fs = [foreign(n) for n in range(3)]
    os, gs = [], []
    for jj, a in ((2, 1), (2, 0), (1, 1), (1, 0)):
        add_relay(jj, a)
    os.append(ours(0, fs[0]))
    add_relay(3, 0)
    line_sum(2, 1)
    os.append(ours(1, fs[1]))
    line_sum(2, 0)
    line_sum(1, 1)
    line_sum(3, 1)
    gs.append(whole(0, os[0]))
    line_sum(1, 0)
    os.append(ours(2, fs[2]))
    line_sum(3, 0)
    gs.append(whole(1, os[1]))
    for a in range(2):
        line_sum(0, a)
    gs.append(whole(2, os[2]))
    for c in qc:
        c.wait_recv()
    qrecv[x * 4 + y] = qout[0]
    table = qrecv[...].reshape(128, 128)
    place8 = lax.broadcasted_iota(jnp.int32, (8, 128), 0)
    probs_out = jnp.zeros((8, 128), F32)
    for k in range(8):
        row = jnp.sum(jnp.where(line == line_of(k), table, 0.0), axis=0, keepdims=True)
        probs_out = jnp.where(place8 == k, row, probs_out)
    pout[...] = probs_out.astype(BF)
    for a in range(2):
        for t in range(2):
            second[a, t, 1].wait_recv()
            second[a, t, 2].wait_recv()
        tout[a * 64:a * 64 + 64, :] = (part(a, 0)[...].astype(F32) + full2[a, 0].astype(F32) + full2[a, 1].astype(F32)).astype(BF)
    for loc, c in gs:
        loc.wait()
        c.wait_recv()
    m2.wait_recv()
    m3.wait_recv()
    done = [c for n in range(8, 16) for c in readers[n]]
    for a in range(2):
        for c in copies[a].values():
            if not any(c is d for d in done):
                c.wait_send()
    for c in list(first.values()) + list(second.values()) + near_in[0] + near_in[1] + fs + os + [c for _, c in gs] + qc:
        c.wait_send()
    for c in [w1, w2, m3, v1, v2] + pc:
        c.wait_send()


def layer(tok, grad, wgu, wdn, mold, vold, routes, probs):
    any_ = pl.BlockSpec(memory_space=pl.ANY)
    vm = pl.BlockSpec(memory_space=pltpu.VMEM)
    sd, dma, V = jax.ShapeDtypeStruct, pltpu.SemaphoreType.DMA, pltpu.VMEM
    return pl.pallas_call(
        layer_kernel,
        name="layer_rows",
        out_shape=(sd((128, 2048), BF), sd((384, 2048), F32), sd((8, 128), BF), sd((4, 2, 384, 2048), BF)),
        in_specs=[any_] * 6 + [vm, vm],
        out_specs=(vm, any_, vm, any_),
        scratch_shapes=[
            V((16, 128, 2048), BF), V((16, 128, 2048), BF), V((16, 8, 128), F32), V((16, 8, 128), F32),
            V((2, 2048, 768), BF), V((2, 384, 2048), BF),
            V((2, 512, 2048), BF), V((2, 512, 2048), BF),
            V((4, 256, 256), BF), V((256, 256), BF), V((2, 512, 128), F32),
            V((256, 768), F32), V((256, 384), F32), V((256, 768), BF), V((512, 384), BF),
            V((2, 384, 2048), F32), V((16, 8, 128), F32),
            V((2, 512, 2048), BF), V((2, 4, 2, 32, 2048), BF), V((2, 4, 2, 64, 2048), BF), V((2, 2, 32, 2048), BF), V((2, 2, 64, 2048), BF),
            V((2, 192, 2048), F32), V((192, 2048), BF), V((192, 2048), BF), V((16, 8, 128), F32),
            dma((3,)), dma((4,)), dma((16,)), dma((16,)), dma((2, 5, 2, 2)), dma((2, 5, 2, 2)), dma((7,)), dma((7,)),
            dma((2, 4, 2, 3)), dma((2, 4, 2, 3)), dma((2, 2, 3)), dma((2, 2, 3)), dma((5, 3)), dma((5, 3)), dma((16,)), dma((16,)),
        ],
        compiler_params=pltpu.CompilerParams(collective_id=0, has_side_effects=True, vmem_limit_bytes=67043328),
    )(tok, grad, wgu, wdn, mold, vold, routes, probs)


def adam_kernel(leader, replicas, g, m, v, mvs, w, tg, pg, down, one, two, tg_out, pg_out, gv, mb, vb, lb, wb, tb, sem, osem, tsem):
    rows, steps = 64, 6
    rank = lax.axis_index("dp")
    lead = leader[0]
    is_lead, is_live = lead == rank, replicas[0, rank] == 1

    def loads(i):
        r = pl.ds(i * rows, rows)
        return (pltpu.make_async_copy(g.at[r], gv.at[r], sem.at[0, i]),
                pltpu.make_async_copy(m.at[0, 0, r], mb.at[r], sem.at[1, i]),
                pltpu.make_async_copy(v.at[0, 0, r], vb.at[r], sem.at[2, i]),
                pltpu.make_async_copy(mvs.at[lead, :, r], lb.at[:, r], sem.at[3, i]),
                pltpu.make_async_copy(w.at[0, r], wb.at[r], sem.at[4, i]))

    def stores(i):
        r = pl.ds(i * rows, rows)
        return (pltpu.make_async_copy(wb.at[r], down.at[0, 0, r], osem.at[0, i]),
                pltpu.make_async_copy(mb.at[r], one.at[0, 0, r], osem.at[1, i]),
                pltpu.make_async_copy(vb.at[r], two.at[0, 0, r], osem.at[2, i]))

    t_in, t_out = pltpu.make_async_copy(tg, tb, tsem), pltpu.make_async_copy(tb, tg_out, tsem)
    for i in range(steps):
        for c in loads(i):
            c.start()
    t_in.start()
    pg_out[...] = pg[...]

    def step(i, _):
        for c in loads(i):
            c.wait()

        def part(t, _):
            r = pl.ds(pl.multiple_of(i * rows + t * 16, 16), 16)
            grad, m_old, v_old, w_old = gv[r], mb[r], vb[r], wb[r]
            m_src = jnp.where(is_lead, m_old, lb[0, r].astype(F32))
            v_src = jnp.where(is_lead, v_old, lb[1, r].astype(F32))
            m_new = beta_one * m_src + (1.0 - beta_one) * grad
            v_new = beta_two * v_src + (1.0 - beta_two) * grad * grad
            m_hat = m_new * (1.0 / (1.0 - beta_one**adam_step))
            v_hat = v_new * (1.0 / (1.0 - beta_two**adam_step))
            w_wide = w_old.astype(F32)
            w_new = (w_wide - learn_rate * (m_hat / (jnp.sqrt(v_hat) + adam_eps) + weight_decay * w_wide)).astype(BF)
            wb[r] = jnp.where(is_live, w_new, w_old)
            mb[r] = jnp.where(is_lead, m_new, m_old)
            vb[r] = jnp.where(is_lead, v_new, v_old)
            return 0

        lax.fori_loop(0, rows // 16, part, 0)
        for c in stores(i):
            c.start()
        return 0

    lax.fori_loop(0, steps, step, 0)
    t_in.wait()
    t_out.start()
    t_out.wait()
    for i in range(steps):
        for c in stores(i):
            c.wait()


def adam(leader, replicas, g, m, v, mvs, w, tg, pg):
    sd, V = jax.ShapeDtypeStruct, pltpu.VMEM
    any_ = pl.BlockSpec(memory_space=pl.ANY)
    return pl.pallas_call(
        adam_kernel,
        name="adam_rows",
        out_shape=(sd((1, 1, 384, 2048), BF), sd((1, 1, 384, 2048), F32), sd((1, 1, 384, 2048), F32), sd((128, 2048), BF), sd((8, 128), BF)),
        in_specs=[pl.BlockSpec(memory_space=pltpu.SMEM)] * 2 + [any_] * 6 + [pl.BlockSpec(memory_space=pltpu.VMEM)],
        out_specs=(any_,) * 4 + (pl.BlockSpec(memory_space=pltpu.VMEM),),
        scratch_shapes=[V((384, 2048), F32), V((384, 2048), F32), V((384, 2048), F32), V((2, 384, 2048), BF), V((384, 2048), BF), V((128, 2048), BF),
                        pltpu.SemaphoreType.DMA((5, 6)), pltpu.SemaphoreType.DMA((3, 6)), pltpu.SemaphoreType.DMA],
    )(leader, replicas, g, m, v, mvs, w, tg, pg)


def body(tokens, out_grad, routes, probs, w_gate_up, w_down, moment_one, moment_two, replicas, leader):
    token_grad, grad, prob_grad, mvs = layer(tokens, out_grad, w_gate_up, w_down, moment_one, moment_two, routes.T, probs.T)
    new_down, new_one, new_two, token_grad, prob_grad = adam(leader, replicas, grad, moment_one, moment_two, mvs, w_down, token_grad, prob_grad)
    return (token_grad, prob_grad.T, new_down, new_one, new_two)


def solution(mesh):
    in_specs = (
        P(("dp", "expert"), None),
        P(("dp", "expert"), None),
        P(("dp", "expert"), None),
        P(("dp", "expert"), None),
        P("expert", None, None),
        P("expert", None, None),
        P("dp", "expert", None, None),
        P("dp", "expert", None, None),
        P("expert", None),
        P("expert"),
    )
    out_specs = (
        P(("dp", "expert"), None),
        P(("dp", "expert"), None),
        P("dp", "expert", None, None),
        P("dp", "expert", None, None),
        P("dp", "expert", None, None),
    )
    return jax.shard_map(body, mesh=mesh, in_specs=in_specs, out_specs=out_specs, check_vma=False)
```

```python
import jax
import jax.numpy as jnp
from jax import lax
from jax.experimental import pallas as pl
from jax.experimental.pallas import tpu as pltpu
from jax.sharding import PartitionSpec as P

F32, BF = jnp.float32, jnp.bfloat16
MESH = pl.DeviceIdType.MESH
learn_rate = 0.01
beta_one = 0.9
beta_two = 0.95
adam_eps = 1e-08
weight_decay = 0.1
adam_step = 100


ORDER = ((0, 0), (3, 0), (1, 0), (0, 3), (0, 1), (3, 3), (3, 1), (1, 3), (1, 1), (2, 0), (0, 2), (3, 2), (1, 2), (2, 3), (2, 1), (2, 2))
SLOT = {p: n for n, p in enumerate(ORDER)}


def slot_of(dx, dy):
    return SLOT[dx % 4, dy % 4]


def nt(a, b):
    return lax.dot_general(a, b, (((1,), (1,)), ((), ())), preferred_element_type=F32)


def tn(a, b):
    return lax.dot_general(a, b, (((0,), (0,)), ((), ())), preferred_element_type=F32)


def place():
    dp = lax.axis_index("dp")
    ex = lax.axis_index("expert")
    return dp // 2, dp % 2, ex // 16, (ex // 4) % 4, ex % 4


def greet(peers):
    barrier = pltpu.get_barrier_semaphore()
    for peer in peers:
        pl.semaphore_signal(barrier, inc=1, device_id=peer, device_id_type=MESH)
    pl.semaphore_wait(barrier, len(peers))


def rdma(src, dst, s, r, peer):
    c = pltpu.make_async_remote_copy(src, dst, s, r, device_id=peer, device_id_type=MESH)
    c.start()
    return c


def layer_kernel(tok, grad, wgu, wdn, mold, vold, routes, probs, tout, gfull, pout, mvs,
                 xs, ds, prec, pst, gus, dns, xc, dc, oall, opall, ps, gu_s, g_s, pre_s, hid_s, gacc, qout,
                 dv, relay, full, relay2, full2, near, frecv, orecv, qrecv,
                 own_sem, w_sem, psend, precv, asend, arecv, wsend, wrecv, s1, r1, s2, r2, ws, wr, qs, qr):
    zl, co, h, x, y = place()
    dp = zl * 2 + co
    me = h * 16 + x * 4 + y

    def at(dx, dy):
        return (dp, h * 16 + ((x + dx) % 4) * 4 + (y + dy) % 4)

    sibling = (zl * 2 + 1 - co, me)
    cross = ((1 - zl) * 2 + co, (1 - h) * 16 + x * 4 + y)
    zside = ((1 - zl) * 2 + co, me)
    inputs, outs = (tok, grad), (xs, ds)
    local = [pltpu.make_async_copy(inputs[a], outs[a].at[0], own_sem.at[a]) for a in range(2)]
    mv_in = [pltpu.make_async_copy(mold.at[0, 0], gacc.at[0], w_sem.at[0]), pltpu.make_async_copy(vold.at[0, 0], gacc.at[1], w_sem.at[1])]
    own_w = [pltpu.make_async_copy(wgu.at[0], gus.at[0], w_sem.at[2]), pltpu.make_async_copy(wdn.at[0], dns.at[0], w_sem.at[3])]
    for c in local + mv_in + own_w:
        c.start()
    greet([at(*ORDER[n]) for n in range(1, 16)] + [sibling, cross, zside])

    rows_gu, rows_dn = pl.ds(co * 1024, 1024), pl.ds(co * 192, 192)
    w1 = rdma(wgu.at[0, rows_gu], gus.at[1, rows_gu], wsend.at[0], wrecv.at[0], cross)
    w2 = rdma(wdn.at[0, rows_dn], dns.at[1, rows_dn], wsend.at[1], wrecv.at[1], cross)

    copies = [{}, {}]
    readers = {n: [] for n in range(16)}
    half = (pl.ds(0, 64), pl.ds(64, 64))

    def rel(a, i, j):
        return (i, j) if a == 0 else (j, i)

    def step(a, t, first):
        s = 1 - 2 * t
        return rel(a, s, 0) if first else rel(a, 0, s)

    def sem_at(i, j, first):
        return 0 if first else 1 + i % 4

    def send(a, i, j, first, t, part):
        d = step(a, t, first)
        bx, by = rel(a, i, j)
        src_slot, dst_slot = slot_of(bx, by), slot_of(bx - d[0], by - d[1])
        k = sem_at(i, j, first)
        p = 0 if part is None else 1
        if part is None:
            src = inputs[a] if (bx, by) == (0, 0) else outs[a].at[src_slot]
            dst = outs[a].at[dst_slot]
        else:
            src, dst = outs[a].at[src_slot, half[part]], outs[a].at[dst_slot, half[part]]
        copies[a][k, t, p] = rdma(src, dst, asend.at[a, k, t, p], arecv.at[a, k, t, p], at(*d))
        if a == 0 and (part is not None or (bx, by) != (0, 0)):
            readers[src_slot].append(copies[a][k, t, p])

    def send_full(a, i, first):
        for t in range(2):
            send(a, i, 0, first, t, None)

    def pass_on(a, i, first):
        k = sem_at(i, 0, first)
        for t in range(2):
            copies[a][k, t, 0].wait_recv()
            s = 2 * t - 1
            if first:
                send(a, s, 0, True, t, t)
            else:
                send(a, i, s, False, t, t)

    def wait_halves(a, i, first):
        k = sem_at(i, 0, first)
        for t in range(2):
            copies[a][k, t, 1].wait_recv()

    for a in range(2):
        send_full(a, 0, True)
    for a in range(2):
        send_full(a, 0, False)
    line = lax.broadcasted_iota(jnp.int32, (128, 128), 0)

    def line_of(k):
        e = routes[k:k + 1, :]
        return (e & 15) * 8 + jnp.where((e >> 4) == h, 0, 1)

    dense = jnp.zeros((128, 128), F32)
    for k in range(8):
        dense = jnp.where(line == line_of(k), probs[k:k + 1, :].astype(F32), dense)
    pst[...] = dense.reshape(16, 8, 128)
    prec[0] = pst[x * 4 + y]
    for c in mv_in:
        c.wait()

    def narrow(t, _):
        rows = pl.ds(pl.multiple_of(t * 64, 64), 64)
        for e in range(2):
            dv[e, rows] = gacc[e, rows].astype(BF)
        return 0

    lax.fori_loop(0, 6, narrow, 0)
    pc = []
    for n in range(1, 16):
        dx, dy = ORDER[n]
        pc.append(rdma(pst.at[((x + dx) % 4) * 4 + (y + dy) % 4], prec.at[slot_of(-dx, -dy)], psend.at[n], precv.at[slot_of(-dx, -dy)], at(dx, dy)))
    dmv = mvs.at[dp]
    m1 = rdma(dv.at[:, pl.ds(0, 384)], dmv, wsend.at[2], wrecv.at[2], zside)
    m2 = rdma(dv.at[:, pl.ds(0, 384)], dmv, wsend.at[3], wrecv.at[3], sibling)
    gacc[...] = jnp.zeros_like(gacc)
    oall[...] = jnp.zeros_like(oall)
    opall[...] = jnp.zeros_like(opall)
    qout[...] = jnp.zeros_like(qout)
    for c in local + own_w:
        c.wait()

    before = (lax.broadcasted_iota(jnp.int32, (128, 128), 0) < lax.broadcasted_iota(jnp.int32, (128, 128), 1)).astype(BF)
    slot = lax.broadcasted_iota(jnp.int32, (64, 128), 0).astype(F32)

    def pack(base, j):
        for i in range(2):
            p = prec[base + j * 2 + i]
            on = (p > 0).astype(F32)
            rank = jnp.dot(on.astype(BF), before, preferred_element_type=F32)
            rank = jnp.where(on > 0, rank, -1.0)
            for e in range(2):
                hot = rank[e:e + 1, :] == slot
                oall[j, pl.ds(e * 128 + i * 64, 64), pl.ds(i * 128, 128)] = hot.astype(F32).astype(BF)
                held = jnp.where(hot, p[e:e + 1, :], 0.0)
                opall[pl.ds(e * 128 + i * 64, 64), pl.ds(i * 128, 128)] = held.astype(BF)
                col = jnp.sum(held, axis=1, keepdims=True)
                ps[e, pl.ds(pl.multiple_of(j * 128 + i * 64, 64), 64), :] = jnp.broadcast_to(col, (64, 128))
        rows = pl.ds(pl.multiple_of(j * 128, 128), 128)
        blocks = pl.ds(base + j * 2, 2)
        for o, src, dst in ((oall[j], xs, xc), (opall[...], ds, dc)):
            r = jnp.dot(o, src[blocks].reshape(256, 2048), preferred_element_type=F32).astype(BF)
            dst[0, rows] = r[:128]
            dst[1, rows] = r[128:]

    def expert(e, tiles):
        def tile(t, _):
            rows = pl.ds(pl.multiple_of(t * 256, 256), 256)
            gu_s[...] = jnp.dot(xc[e, rows], gus[e], preferred_element_type=F32)
            g_s[...] = nt(dc[e, rows], dns[e])
            gate, up, g = gu_s[:, :384], gu_s[:, 384:], g_s[...]
            p = ps[e, rows, :1]
            sig = 0.5 * jnp.tanh(0.5 * gate) + 0.5
            silu = gate * sig
            hid = (silu * up).astype(BF)
            q = jnp.sum(hid.astype(F32) * g, axis=1, keepdims=True) / jnp.where(p > 0, p, 1.0)
            hid_s[rows] = hid
            pre_s[:, :384] = (g * up * (sig * (1.0 + gate * (1.0 - sig)))).astype(BF)
            pre_s[:, 384:] = (g * silu).astype(BF)
            ps[e, rows, :] = jnp.broadcast_to(q, (256, 128))
            xc[e, rows] = nt(pre_s[...], gus[e]).astype(BF)
            return 0

        lax.fori_loop(0, tiles, tile, 0)
        n = tiles * 256
        gacc[e] += tn(hid_s[:n], dc[e, :n])

    def spread(base, j):
        rows = pl.ds(pl.multiple_of(j * 128, 128), 128)
        o = oall[j]
        r = tn(o[:128], xc[0, rows]) + tn(o[128:], xc[1, rows])
        if base == 0:
            dv[j // 2, pl.ds(pl.multiple_of(j % 2 * 256, 256), 256)] = r.astype(BF)
        else:
            xs[pl.ds(base + j * 2, 2)] = r.astype(BF).reshape(2, 128, 2048)
        for i in range(2):
            for e in range(2):
                hot = oall[j, pl.ds(e * 128 + i * 64, 64), pl.ds(i * 128, 128)].astype(F32)
                q = ps[e, pl.ds(pl.multiple_of(j * 128 + i * 64, 64), 64), :]
                qout[base + j * 2 + i, e:e + 1, :] = jnp.sum(hot * q, axis=0, keepdims=True)

    def loop(n, f, base):
        def go(j, _):
            f(base, j)
            return 0
        lax.fori_loop(0, n, go, 0)

    order = (2, 1, 3, 0)
    quarter = (pl.ds(0, 32), pl.ds(32, 32))
    first, second = {}, {}
    qc = []

    def spot(a, i, j):
        return slot_of(*rel(a, i, j))

    def sums(n):
        return dv.at[n // 4, pl.ds(n % 4 * 128, 128)] if n < 8 else xs.at[n]

    def give(lo, hi):
        for kind in range(2):
            for jj in order:
                for a in range(2):
                    for t in range(2):
                        peer = at(*rel(a, 1 - 2 * t, 0))
                        b = spot(a, 2 if kind == 0 else 1 - 2 * t, jj)
                        if not lo <= b < hi:
                            continue
                        if kind == 0:
                            src, dst = sums(b).at[pl.ds(a * 64 + t * 32, 32)], relay.at[a, jj, t]
                        else:
                            src, dst = sums(b).at[pl.ds(a * 64 + (1 - t) * 32, 32)], full.at[a, jj, t, quarter[1 - t]]
                        first[a, jj, t, kind] = rdma(src, dst, s1.at[a, jj, t, kind], r1.at[a, jj, t, kind], peer)
        for n in range(max(lo, 1), hi):
            dx, dy = ORDER[n]
            back = slot_of(-dx, -dy)
            qc.append(rdma(qout.at[n], qrecv.at[x * 4 + y], qs.at[n], qr.at[back], at(dx, dy)))

    def spread_all(base, pairs):
        for n in range(max(base, 8), base + 2 * pairs):
            for c in readers[n]:
                c.wait_send()
        loop(pairs, spread, base)

    def add_relay(jj, a):
        for t in range(2):
            first[a, jj, t, 0].wait_recv()
            to = spot(a, 1 - 2 * t, jj)
            lo = a * 64 + t * 32
            relay[a, jj, t] = (relay[a, jj, t].astype(F32) + sums(to)[lo:lo + 32].astype(F32)).astype(BF)
            first[a, jj, t, 2] = rdma(relay.at[a, jj, t], full.at[a, jj, t, quarter[t]], s1.at[a, jj, t, 2], r1.at[a, jj, t, 2], at(*rel(a, 1 - 2 * t, 0)))

    def part(a, jj):
        return xc.at[a, pl.ds(jj * 64, 64)]

    def line_sum(jj, a):
        for t in range(2):
            first[a, jj, t, 1].wait_recv()
            first[a, jj, t, 2].wait_recv()
        here = spot(a, 0, jj)
        mine = part(a, jj)
        mine[...] = (sums(here)[a * 64:a * 64 + 64].astype(F32) + full[a, jj, 0].astype(F32) + full[a, jj, 1].astype(F32)).astype(BF)
        side = [at(*rel(a, 0, 1 - 2 * t)) for t in range(2)]
        if jj == 2:
            for t in range(2):
                second[a, t, 0] = rdma(mine.at[quarter[t]], relay2.at[a, t], s2.at[a, t, 0], r2.at[a, t, 0], side[t])
        elif jj != 0:
            t = 0 if jj == 1 else 1
            second[a, t, 1] = rdma(mine.at[quarter[1 - t]], full2.at[a, t, quarter[1 - t]], s2.at[a, t, 1], r2.at[a, t, 1], side[t])
            second[a, t, 0].wait_recv()
            relay2[a, t] = (relay2[a, t].astype(F32) + mine[t * 32:t * 32 + 32].astype(F32)).astype(BF)
            second[a, t, 2] = rdma(relay2.at[a, t], full2.at[a, t, quarter[t]], s2.at[a, t, 2], r2.at[a, t, 2], side[t])

    near_in = [[None] * 3 for _ in range(2)]

    def halves(e):
        for n in range(3):
            near_in[e][n] = rdma(gacc.at[e, pl.ds((1 - co) * 192 + n * 64, 64)], near.at[e, pl.ds(n * 64, 64)], ws.at[e, n], wr.at[e, n], sibling)

    def rows_of(n):
        return pl.ds(pl.multiple_of(co * 192 + n * 64, 64), 64), pl.ds(n * 64, 64)

    def foreign(n):
        mine, rows = rows_of(n)
        near_in[1][n].wait_recv()
        xc[0, pl.ds(256 + n * 64, 64)] = (gacc[1, mine] + near[1, rows]).astype(BF)
        return rdma(xc.at[0, pl.ds(256 + n * 64, 64)], frecv.at[rows], ws.at[2, n], wr.at[2, n], cross)

    def ours(n, f):
        mine, rows = rows_of(n)
        near_in[0][n].wait_recv()
        f.wait_recv()
        v = gacc[0, mine] + near[0, rows] + frecv[rows].astype(F32)
        gacc[0, mine] = v
        xc[1, pl.ds(256 + n * 64, 64)] = v.astype(BF)
        return rdma(xc.at[1, pl.ds(256 + n * 64, 64)], orecv.at[rows], ws.at[3, n], wr.at[3, n], zside)

    def whole(n, o):
        mine, rows = rows_of(n)
        o.wait_recv()
        gacc[0, mine] = gacc[0, mine] + orecv[rows].astype(F32)
        loc = pltpu.make_async_copy(gacc.at[0, mine], gfull.at[mine], w_sem.at[n])
        loc.start()
        return loc, rdma(gacc.at[0, mine], gfull.at[mine], ws.at[4, n], wr.at[4, n], sibling)

    for a in range(2):
        pass_on(a, 0, True)
    for i in (3, 1):
        for a in range(2):
            send_full(a, i, False)
    for a in range(2):
        pass_on(a, 0, False)
    for a in range(2):
        wait_halves(a, 0, True)
    for a in range(2):
        send_full(a, 2, False)
    for c in pc:
        c.wait_recv()
    loop(2, pack, 0)
    for i in (3, 1):
        for a in range(2):
            pass_on(a, i, False)

    def late(j, _):
        pack(0, j + 2)
        return 0

    lax.fori_loop(0, 2, late, 0)
    w1.wait_recv()
    v1 = rdma(gus.at[1, rows_gu], gus.at[1, rows_gu], wsend.at[4], wrecv.at[4], sibling)
    w2.wait_recv()
    v2 = rdma(dns.at[1, rows_dn], dns.at[1, rows_dn], wsend.at[5], wrecv.at[5], sibling)
    expert(0, 2)
    v1.wait_recv()
    v2.wait_recv()
    expert(1, 2)
    for a in range(2):
        pass_on(a, 2, False)
    for c in (m1, m2):
        c.wait_send()
    spread_all(0, 4)
    m1.wait_recv()
    zdp = (1 - zl) * 2 + co
    m3 = rdma(mvs.at[zdp], mvs.at[zdp], wsend.at[6], wrecv.at[6], sibling)
    for i in (0, 3):
        for a in range(2):
            wait_halves(a, i, False)
    loop(2, pack, 8)
    for e in range(2):
        expert(e, 1)
    spread_all(8, 2)
    for i in (1, 2):
        for a in range(2):
            wait_halves(a, i, False)
    give(8, 12)
    give(0, 8)
    loop(2, pack, 12)
    expert(1, 1)
    halves(1)
    for jj, a in ((0, 0), (0, 1), (3, 1)):
        add_relay(jj, a)
    expert(0, 1)
    halves(0)
    spread_all(12, 2)
    give(12, 16)
    fs = [foreign(n) for n in range(3)]
    os, gs = [], []
    for jj, a in ((2, 1), (2, 0), (1, 1), (1, 0)):
        add_relay(jj, a)
    os.append(ours(0, fs[0]))
    add_relay(3, 0)
    line_sum(2, 1)
    os.append(ours(1, fs[1]))
    line_sum(2, 0)
    line_sum(1, 1)
    line_sum(3, 1)
    gs.append(whole(0, os[0]))
    line_sum(1, 0)
    os.append(ours(2, fs[2]))
    line_sum(3, 0)
    gs.append(whole(1, os[1]))
    for a in range(2):
        line_sum(0, a)
    gs.append(whole(2, os[2]))
    for c in qc:
        c.wait_recv()
    qrecv[x * 4 + y] = qout[0]
    table = qrecv[...].reshape(128, 128)
    place8 = lax.broadcasted_iota(jnp.int32, (8, 128), 0)
    probs_out = jnp.zeros((8, 128), F32)
    for k in range(8):
        row = jnp.sum(jnp.where(line == line_of(k), table, 0.0), axis=0, keepdims=True)
        probs_out = jnp.where(place8 == k, row, probs_out)
    pout[...] = probs_out.astype(BF)
    for a in range(2):
        for t in range(2):
            second[a, t, 1].wait_recv()
            second[a, t, 2].wait_recv()
        tout[a * 64:a * 64 + 64, :] = (part(a, 0)[...].astype(F32) + full2[a, 0].astype(F32) + full2[a, 1].astype(F32)).astype(BF)
    for loc, c in gs:
        loc.wait()
        c.wait_recv()
    m2.wait_recv()
    m3.wait_recv()
    done = [c for n in range(8, 16) for c in readers[n]]
    for a in range(2):
        for c in copies[a].values():
            if not any(c is d for d in done):
                c.wait_send()
    for c in list(first.values()) + list(second.values()) + near_in[0] + near_in[1] + fs + os + [c for _, c in gs] + qc:
        c.wait_send()
    for c in [w1, w2, m3, v1, v2] + pc:
        c.wait_send()


def layer(tok, grad, wgu, wdn, mold, vold, routes, probs):
    any_ = pl.BlockSpec(memory_space=pl.ANY)
    vm = pl.BlockSpec(memory_space=pltpu.VMEM)
    sd, dma, V = jax.ShapeDtypeStruct, pltpu.SemaphoreType.DMA, pltpu.VMEM
    return pl.pallas_call(
        layer_kernel,
        name="layer_rows",
        out_shape=(sd((128, 2048), BF), sd((384, 2048), F32), sd((8, 128), BF), sd((4, 2, 384, 2048), BF)),
        in_specs=[any_] * 6 + [vm, vm],
        out_specs=(vm, any_, vm, any_),
        scratch_shapes=[
            V((16, 128, 2048), BF), V((16, 128, 2048), BF), V((16, 8, 128), F32), V((16, 8, 128), F32),
            V((2, 2048, 768), BF), V((2, 384, 2048), BF),
            V((2, 512, 2048), BF), V((2, 512, 2048), BF),
            V((4, 256, 256), BF), V((256, 256), BF), V((2, 512, 128), F32),
            V((256, 768), F32), V((256, 384), F32), V((256, 768), BF), V((512, 384), BF),
            V((2, 384, 2048), F32), V((16, 8, 128), F32),
            V((2, 512, 2048), BF), V((2, 4, 2, 32, 2048), BF), V((2, 4, 2, 64, 2048), BF), V((2, 2, 32, 2048), BF), V((2, 2, 64, 2048), BF),
            V((2, 192, 2048), F32), V((192, 2048), BF), V((192, 2048), BF), V((16, 8, 128), F32),
            dma((3,)), dma((4,)), dma((16,)), dma((16,)), dma((2, 5, 2, 2)), dma((2, 5, 2, 2)), dma((7,)), dma((7,)),
            dma((2, 4, 2, 3)), dma((2, 4, 2, 3)), dma((2, 2, 3)), dma((2, 2, 3)), dma((5, 3)), dma((5, 3)), dma((16,)), dma((16,)),
        ],
        compiler_params=pltpu.CompilerParams(collective_id=0, has_side_effects=True, vmem_limit_bytes=67043328),
    )(tok, grad, wgu, wdn, mold, vold, routes, probs)


def adam_kernel(leader, replicas, g, m, v, mvs, w, tg, pg, down, one, two, tg_out, pg_out, gv, mb, vb, lb, wb, tb, sem, osem, tsem):
    rows, steps = 64, 6
    rank = lax.axis_index("dp")
    lead = leader[0]
    is_lead, is_live = lead == rank, replicas[0, rank] == 1

    def loads(i):
        r = pl.ds(i * rows, rows)
        return (pltpu.make_async_copy(g.at[r], gv.at[r], sem.at[0, i]),
                pltpu.make_async_copy(m.at[0, 0, r], mb.at[r], sem.at[1, i]),
                pltpu.make_async_copy(v.at[0, 0, r], vb.at[r], sem.at[2, i]),
                pltpu.make_async_copy(mvs.at[lead, :, r], lb.at[:, r], sem.at[3, i]),
                pltpu.make_async_copy(w.at[0, r], wb.at[r], sem.at[4, i]))

    def stores(i):
        r = pl.ds(i * rows, rows)
        return (pltpu.make_async_copy(wb.at[r], down.at[0, 0, r], osem.at[0, i]),
                pltpu.make_async_copy(mb.at[r], one.at[0, 0, r], osem.at[1, i]),
                pltpu.make_async_copy(vb.at[r], two.at[0, 0, r], osem.at[2, i]))

    t_in, t_out = pltpu.make_async_copy(tg, tb, tsem), pltpu.make_async_copy(tb, tg_out, tsem)
    for i in range(steps):
        for c in loads(i):
            c.start()
    t_in.start()
    pg_out[...] = pg[...]

    def step(i, _):
        for c in loads(i):
            c.wait()

        def part(t, _):
            r = pl.ds(pl.multiple_of(i * rows + t * 16, 16), 16)
            grad, m_old, v_old, w_old = gv[r], mb[r], vb[r], wb[r]
            m_src = jnp.where(is_lead, m_old, lb[0, r].astype(F32))
            v_src = jnp.where(is_lead, v_old, lb[1, r].astype(F32))
            m_new = beta_one * m_src + (1.0 - beta_one) * grad
            v_new = beta_two * v_src + (1.0 - beta_two) * grad * grad
            m_hat = m_new * (1.0 / (1.0 - beta_one**adam_step))
            v_hat = v_new * (1.0 / (1.0 - beta_two**adam_step))
            w_wide = w_old.astype(F32)
            w_new = (w_wide - learn_rate * (m_hat / (jnp.sqrt(v_hat) + adam_eps) + weight_decay * w_wide)).astype(BF)
            wb[r] = jnp.where(is_live, w_new, w_old)
            mb[r] = jnp.where(is_lead, m_new, m_old)
            vb[r] = jnp.where(is_lead, v_new, v_old)
            return 0

        lax.fori_loop(0, rows // 16, part, 0)
        for c in stores(i):
            c.start()
        return 0

    lax.fori_loop(0, steps, step, 0)
    t_in.wait()
    t_out.start()
    t_out.wait()
    for i in range(steps):
        for c in stores(i):
            c.wait()


def adam(leader, replicas, g, m, v, mvs, w, tg, pg):
    sd, V = jax.ShapeDtypeStruct, pltpu.VMEM
    any_ = pl.BlockSpec(memory_space=pl.ANY)
    return pl.pallas_call(
        adam_kernel,
        name="adam_rows",
        out_shape=(sd((1, 1, 384, 2048), BF), sd((1, 1, 384, 2048), F32), sd((1, 1, 384, 2048), F32), sd((128, 2048), BF), sd((8, 128), BF)),
        in_specs=[pl.BlockSpec(memory_space=pltpu.SMEM)] * 2 + [any_] * 6 + [pl.BlockSpec(memory_space=pltpu.VMEM)],
        out_specs=(any_,) * 4 + (pl.BlockSpec(memory_space=pltpu.VMEM),),
        scratch_shapes=[V((384, 2048), F32), V((384, 2048), F32), V((384, 2048), F32), V((2, 384, 2048), BF), V((384, 2048), BF), V((128, 2048), BF),
                        pltpu.SemaphoreType.DMA((5, 6)), pltpu.SemaphoreType.DMA((3, 6)), pltpu.SemaphoreType.DMA],
    )(leader, replicas, g, m, v, mvs, w, tg, pg)


def body(tokens, out_grad, routes, probs, w_gate_up, w_down, moment_one, moment_two, replicas, leader):
    token_grad, grad, prob_grad, mvs = layer(tokens, out_grad, w_gate_up, w_down, moment_one, moment_two, routes.T, probs.T)
    new_down, new_one, new_two, token_grad, prob_grad = adam(leader, replicas, grad, moment_one, moment_two, mvs, w_down, token_grad, prob_grad)
    return (token_grad, prob_grad.T, new_down, new_one, new_two)


def solution(mesh):
    in_specs = (
        P(("dp", "expert"), None),
        P(("dp", "expert"), None),
        P(("dp", "expert"), None),
        P(("dp", "expert"), None),
        P("expert", None, None),
        P("expert", None, None),
        P("dp", "expert", None, None),
        P("dp", "expert", None, None),
        P("expert", None),
        P("expert"),
    )
    out_specs = (
        P(("dp", "expert"), None),
        P(("dp", "expert"), None),
        P("dp", "expert", None, None),
        P("dp", "expert", None, None),
        P("dp", "expert", None, None),
    )
    return jax.shard_map(body, mesh=mesh, in_specs=in_specs, out_specs=out_specs, check_vma=False)
```
